768 devices in a mesh: seq: 96 (over z, x, core), head: 8 (over y).
Axes of the slice: x: 4, y: 8, z: 12, core: 2. Of those that a mesh axis runs over, the one named last changes fastest.
Arguments:
- tokens: bfloat16 [24576, 2048], P('seq'), may hold values from -6 to 6
- q_weight: bfloat16 [2048, 4096], P(None, 'head'), may hold values from -0.125 to 0.125
- gate_weight: bfloat16 [2048, 4096], P(None, 'head'), may hold values from -0.125 to 0.125
- k_weight: bfloat16 [2048, 512], replicated, may hold values from -0.125 to 0.125
- v_weight: bfloat16 [2048, 512], replicated, may hold values from -0.125 to 0.125
- q_gain: float32 [256], replicated, may hold values from 0.1 to 1.9
- k_gain: float32 [256], replicated, may hold values from 0.1 to 1.9
- out_weight: bfloat16 [4096, 2048], P('head'), may hold values from -0.09375 to 0.09375
- doc_starts: int32 [48], replicated, may hold values from 0 to 24575, as said below
- readers: int32 [96, 3], replicated, may hold values from 0 to 1, as said below
Outputs:
- attended: bfloat16 [24576, 2048], P(('seq', 'head'))
The draws below stay inside these ranges and needn't reach their ends.
Inputs may be any that keep to these rules, and one draw needn't show every extreme that they name: doc_starts[0] = 0, doc_starts[47] = 24575, and for m >= 1 doc_starts[m] lies in [m * 512, (m + 1) * 512); every document has 1 to 1023 tokens, and one has exactly 1023 and starts at a multiple of 256. readers[j, s - 1] is 1 exactly when block j and block j + s (s = 1 to 3, j + s below 96) hold tokens of one document, as given by doc_starts; some block has a reader at distance 3.
All inputs are finite; a program needn't handle non-finite values.
Results may differ from the reference program's by a relative error of at most 0.015.
Values may be sent and summed in bfloat16 or wider, within the bound.
No kernel may reach another device: no remote copies, remote signals or barrier semaphores. Data moves between devices by JAX's collectives and lax.ppermute only.
A program may use at most 64 MiB of HBM per device.

```python
import jax
import jax.numpy as jnp
from jax import lax

D = 2048
HEADS = 16
KV_HEADS = 2
HD = 256
TOK_DEV = 256
SPAN = 3
STEP = 512
BLOCKS = 96
DOCS = 48
TOKENS = 24576


def start_table(key):
    sub_key = jax.random.fold_in(key, 4242)
    jitter = jax.random.randint(jax.random.fold_in(sub_key, 1), (DOCS - 1,), 0, STEP)
    chosen = jax.random.randint(jax.random.fold_in(sub_key, 2), (), 0, DOCS - 1)
    slot_ids = jnp.arange(DOCS - 1)
    jitter = jnp.where(slot_ids == chosen, STEP - 1, jnp.where(slot_ids == chosen - 1, 0, jitter))
    jitter = jnp.where(slot_ids == DOCS - 2, STEP - 1, jitter)
    cut_points = (slot_ids + 1) * STEP + jitter
    return jnp.concatenate([jnp.zeros((1,), jnp.int32), cut_points.astype(jnp.int32)])


def draw_doc_starts(key, part):
    return start_table(key)


def draw_readers(key, part):
    starts = start_table(key)
    firsts = jnp.arange(BLOCKS, dtype=jnp.int32) * TOK_DEV
    last_rows = firsts + TOK_DEV - 1
    first_doc = jnp.sum((starts[None, :] <= firsts[:, None]).astype(jnp.int32), axis=1)
    last_doc = jnp.sum((starts[None, :] <= last_rows[:, None]).astype(jnp.int32), axis=1)
    later_blocks = jnp.arange(BLOCKS, dtype=jnp.int32)[:, None] + jnp.arange(1, SPAN + 1, dtype=jnp.int32)[None, :]
    inside = later_blocks < BLOCKS
    target = first_doc[jnp.minimum(later_blocks, BLOCKS - 1)]
    return jnp.where(inside & (target == last_doc[:, None]), 1, 0).astype(jnp.int32)


def shard_levels(rng, shape, split, smallest, top_value):
    level = 1.0
    for axis_at, parts in split:
        draws = jax.random.uniform(jax.random.fold_in(jax.random.fold_in(rng, 6), axis_at), (parts,), jnp.float32, smallest / len(split), top_value / len(split))
        level = level * jnp.repeat(jnp.exp(draws), shape[axis_at] // parts).reshape((-1,) + (1,) * (len(shape) - 1 - axis_at))
    return level


def normal_values(own_key, extent, width, reach, pieces=(), held_as=jnp.bfloat16):
    gain = shard_levels(own_key, extent, pieces, -0.22, 0.18) if pieces else 1.0
    drawn = jax.random.normal(own_key, extent, jnp.float32) * width * gain
    return jnp.minimum(jnp.maximum(drawn, -reach), reach).astype(held_as)


def setup_inputs(seed: int = 0) -> dict:
    seeds = jax.random.split(jax.random.key(seed), 11)
    return {
        "tokens": normal_values(seeds[0], (TOKENS, D), 1.0, 6.0, ((0, 96),)),
        "q_weight": normal_values(seeds[1], (D, HEADS * HD), D ** -0.5, 0.125, ((1, 8),)),
        "gate_weight": normal_values(seeds[2], (D, HEADS * HD), D ** -0.5, 0.125, ((1, 8),)),
        "k_weight": normal_values(seeds[3], (D, KV_HEADS * HD), D ** -0.5, 0.125),
        "v_weight": normal_values(seeds[4], (D, KV_HEADS * HD), D ** -0.5, 0.125),
        "q_gain": jnp.clip(1.0 + 0.18 * jax.random.normal(seeds[5], (HD,), jnp.float32), 0.1, 1.9),
        "k_gain": jnp.clip(1.0 + 0.18 * jax.random.normal(seeds[6], (HD,), jnp.float32), 0.1, 1.9),
        "out_weight": normal_values(seeds[7], (HEADS * HD, D), (HEADS * HD) ** -0.5, 0.09375, ((0, 8),)),
        "doc_starts": draw_doc_starts(jax.random.fold_in(seeds[10], 71), 0),
        "readers": draw_readers(jax.random.fold_in(seeds[10], 71), 0),
    }


ROPE_THETA = 10000000.0
EPSILON = 1e-06

def normed(head_values, gain_vector):
    mean_square = lax.optimization_barrier(jnp.mean(head_values * head_values, axis=-1, keepdims=True))
    return head_values * lax.rsqrt(mean_square + EPSILON) * gain_vector

def rotated(head_values, doc_offsets):
    rot_width = head_values.shape[-1] // 4
    rot_half = rot_width // 2
    frequency = ROPE_THETA ** (-(jnp.arange(rot_half, dtype=jnp.float32) * 2.0 / rot_width))
    angles = doc_offsets[:, None] * frequency[None, :]
    cosine = jnp.cos(angles)[:, None, :]
    sine_part = jnp.sin(angles)[:, None, :]
    front_part = head_values[..., :rot_half]
    back_part = head_values[..., rot_half:rot_width]
    return jnp.concatenate([front_part * cosine - back_part * sine_part, back_part * cosine + front_part * sine_part, head_values[..., rot_width:]], axis=-1)

def locate(doc_starts, positions):
    before = doc_starts[None, :] <= positions[:, None]
    doc_index = lax.optimization_barrier(jnp.sum(before.astype(jnp.int32), axis=1))
    doc_begin = lax.optimization_barrier(jnp.max(jnp.where(before, doc_starts[None, :], 0), axis=1))
    return (doc_index, positions - doc_begin)

def reference(tokens, q_weight, gate_weight, k_weight, v_weight, q_gain, k_gain, out_weight, doc_starts, readers):
    positions = jnp.arange(TOKENS, dtype=jnp.int32)
    doc_ids, offsets = locate(doc_starts, positions)
    offsets_float = offsets.astype(jnp.float32)
    queries = jnp.dot(tokens, q_weight, preferred_element_type=jnp.float32).reshape(TOKENS, HEADS, HD)
    queries = rotated(normed(queries, q_gain), offsets_float).astype(jnp.bfloat16)
    key_rows = jnp.dot(tokens, k_weight, preferred_element_type=jnp.float32).reshape(TOKENS, KV_HEADS, HD)
    key_rows = rotated(normed(key_rows, k_gain), offsets_float).astype(jnp.bfloat16)
    value_rows = jnp.dot(tokens, v_weight, preferred_element_type=jnp.float32).astype(jnp.bfloat16).reshape(TOKENS, KV_HEADS, HD)
    gate_logits = jnp.dot(tokens, gate_weight, preferred_element_type=jnp.float32)
    group_size = HEADS // KV_HEADS
    score_scale = HD ** (-0.5)

    def one_block(block_id):
        row_start = block_id * TOK_DEV
        query_block = lax.dynamic_slice_in_dim(queries, row_start, TOK_DEV, 0).astype(jnp.float32)
        query_block = query_block.reshape(TOK_DEV, KV_HEADS, group_size, HD)
        query_positions = row_start + jnp.arange(TOK_DEV, dtype=jnp.int32)
        query_docs = lax.dynamic_slice_in_dim(doc_ids, row_start, TOK_DEV, 0)
        numerator = jnp.zeros((TOK_DEV, KV_HEADS, group_size, HD), jnp.float32)
        denominator = jnp.zeros((TOK_DEV, KV_HEADS, group_size), jnp.float32)
        for distance in range(SPAN + 1):
            source = block_id - distance
            safe_source = jnp.maximum(source, 0)
            key_start = (safe_source * TOK_DEV).astype(jnp.int32)
            key_block = lax.dynamic_slice_in_dim(key_rows, key_start, TOK_DEV, 0).astype(jnp.float32)
            value_block = lax.dynamic_slice_in_dim(value_rows, key_start, TOK_DEV, 0).astype(jnp.float32)
            key_positions = key_start + jnp.arange(TOK_DEV, dtype=jnp.int32)
            key_docs = lax.dynamic_slice_in_dim(doc_ids, key_start, TOK_DEV, 0)
            if distance == 0:
                listed = source >= 0
            else:
                listed = (source >= 0) & (readers[safe_source, distance - 1] == 1)
            allowed = (query_docs[:, None] == key_docs[None, :]) & (key_positions[None, :] <= query_positions[:, None])

            def accumulate(totals, key_block=key_block, value_block=value_block, allowed=allowed):
                scores = jnp.einsum('tcgd,ucd->tcgu', query_block, key_block) * score_scale
                weights = jnp.where(allowed[:, None, None, :], jnp.exp(scores), 0.0).astype(jnp.bfloat16)
                weights = lax.optimization_barrier(weights).astype(jnp.float32)
                return (totals[0] + jnp.einsum('tcgu,ucd->tcgd', weights, value_block), totals[1] + lax.optimization_barrier(jnp.sum(weights, axis=-1)))
            numerator, denominator = lax.cond(listed, accumulate, lambda totals: totals, (numerator, denominator))
        attention = (numerator / denominator[..., None]).reshape(TOK_DEV, HEADS, HD)
        gate_block = lax.dynamic_slice_in_dim(gate_logits, row_start, TOK_DEV, 0).reshape(TOK_DEV, HEADS, HD)
        mixed_heads = (attention * jax.nn.sigmoid(gate_block)).astype(jnp.bfloat16).reshape(TOK_DEV, HEADS * HD)
        return jnp.dot(mixed_heads, out_weight, preferred_element_type=jnp.float32).astype(jnp.bfloat16)
    return lax.map(one_block, jnp.arange(BLOCKS, dtype=jnp.int32)).reshape(TOKENS, D)
```

```python
import functools

import jax
import jax.numpy as jnp
import numpy as np
from jax import lax
from jax.experimental import pallas as pl
from jax.experimental.pallas import tpu as pltpu
from jax.sharding import PartitionSpec as P

HEADS = 16
ROPE_THETA = 10000000.0
EPSILON = 1e-06

F32 = jnp.float32
BF16 = jnp.bfloat16
ANY = pl.BlockSpec(memory_space=pl.ANY)
VMEM = pl.BlockSpec(memory_space=pltpu.VMEM)
SMEM = pl.BlockSpec(memory_space=pltpu.SMEM)


def params(mib):
    return pltpu.CompilerParams(vmem_limit_bytes=mib << 20)


def cost(flops, nbytes, trans=0):
    return pl.CostEstimate(flops=flops, bytes_accessed=nbytes, transcendentals=trans)


def rope_rows(head_dim):
    rot_width = head_dim // 4
    half = rot_width // 2
    frequency = ROPE_THETA ** (-(np.arange(half, dtype=np.float64) * 2.0 / rot_width))
    rows = np.zeros((8, 128), np.float32)
    rows[0, :half] = frequency
    rows[0, half:rot_width] = frequency
    rows[1, :half] = -1.0
    rows[1, half:rot_width] = 1.0
    return rows


def doc_begin(starts, rows, base):
    at = base + lax.broadcasted_iota(jnp.int32, (rows, starts.shape[1]), 0)
    return jnp.max(jnp.where(starts <= at, starts, 0), axis=1, keepdims=True)


def normed_rotated(x, gain, cosine, sine, half):
    square = jnp.mean(x * x, axis=-1, keepdims=True)
    x = x * lax.rsqrt(square + EPSILON) * gain
    front = x[:, :128]
    lane = lax.broadcasted_iota(jnp.int32, front.shape, 1)
    partner = jnp.where(
        lane < half, pltpu.roll(front, 128 - half, 1), pltpu.roll(front, half, 1)
    )
    return front * cosine + partner * sine, x[:, 128:]


def kv_body(head_dim, kv_share, starts, rope, gain, tok_in, kw_in, vw_in, kv, trig, tok, kw, vw, sems):
    rows = tok.shape[0]
    column = pl.multiple_of((lax.axis_index("head") // kv_share) * head_dim, head_dim)
    columns = pl.ds(column, head_dim)
    copies = [
        pltpu.make_async_copy(tok_in, tok, sems.at[0]),
        pltpu.make_async_copy(kw_in.at[:, columns], kw, sems.at[1]),
        pltpu.make_async_copy(vw_in.at[:, columns], vw, sems.at[2]),
    ]
    for c in copies:
        c.start()
    base = lax.axis_index("seq") * rows
    begin = doc_begin(starts[...], rows, base)
    offset = (base + lax.broadcasted_iota(jnp.int32, (rows, 1), 0) - begin).astype(F32)
    angle = offset * rope[0:1, :]
    cosine = jnp.cos(angle)
    sine = jnp.sin(angle) * rope[1:2, :]
    trig[:, :128] = cosine
    trig[:, 128:] = sine
    copies[0].wait()
    copies[1].wait()
    key = jnp.dot(tok[...], kw[...], preferred_element_type=F32)
    front, back = normed_rotated(key, gain[...], cosine, sine, head_dim // 8)
    kv[:, :128] = front.astype(BF16)
    kv[:, 128:head_dim] = back.astype(BF16)
    copies[2].wait()
    kv[:, head_dim:] = jnp.dot(tok[...], vw[...], preferred_element_type=F32).astype(BF16)


def attend(query, key, value, keep, scale):
    scores = lax.dot_general(query, key, (((1,), (1,)), ((), ())), preferred_element_type=F32)
    weights = jnp.where(keep, jnp.exp(scores * scale), 0.0).astype(BF16)
    wide = weights.astype(F32)
    half = wide.shape[1] // 2
    return (
        jnp.dot(weights, value, preferred_element_type=F32),
        wide[:, :half] + wide[:, half:],
    )


def kept(rows, width, query_base, key_base, begin):
    at = query_base + lax.broadcasted_iota(jnp.int32, (rows, width), 0)
    key = key_base + lax.broadcasted_iota(jnp.int32, (rows, width), 1)
    return (key <= at) & (key >= begin)


def q_body(head_dim, starts, gain, trig, kv, tok_in, qw_in, gw_in, q_out, gate, num, den, tok, w, sems):
    rows = tok.shape[0]
    heads = qw_in.shape[1] // head_dim
    token_copy = pltpu.make_async_copy(tok_in, tok, sems.at[2 * heads])
    token_copy.start()
    copies = []
    for i in range(2 * heads):
        source = qw_in if i < heads else gw_in
        columns = pl.ds((i % heads) * head_dim, head_dim)
        copies.append(pltpu.make_async_copy(source.at[:, columns], w.at[i], sems.at[i]))
        copies[i].start()
    base = lax.axis_index("seq") * rows
    begin = doc_begin(starts[...], rows, base)
    keep = kept(rows, rows, base, base, begin)
    token_copy.wait()
    for i in range(heads):
        at = pl.ds(i * rows, rows)
        copies[i].wait()
        query = jnp.dot(tok[...], w[i], preferred_element_type=F32)
        front, back = normed_rotated(query, gain[...], trig[:, :128], trig[:, 128:], head_dim // 8)
        q_out[at, :128] = front.astype(BF16)
        q_out[at, 128:] = back.astype(BF16)
        weighted, sums = attend(
            q_out[at, :], kv[:, :head_dim], kv[:, head_dim:], keep, head_dim ** (-0.5)
        )
        num[at, :] = weighted
        den[at, :] = sums
    for i in range(heads):
        copies[heads + i].wait()
        logits = jnp.dot(tok[...], w[heads + i], preferred_element_type=F32)
        gate[pl.ds(i * rows, rows), :] = 1.0 / (1.0 + jnp.exp(-logits))


def out_body(head_dim, starts, readers, query, gate, num, den, near, far, own, ow, parts, gated, turned):
    heads = query.shape[0] // head_dim
    rows = query.shape[0] // heads
    block = lax.axis_index("seq")
    core = lax.rem(block, 2)
    head = lax.axis_index("head")
    base = block * rows
    begin = doc_begin(starts[...], rows, base)
    chip = block - core

    def mask(source):
        distance = block - source
        inside = (source >= 0) & (distance >= 1) & (distance <= readers.shape[0])
        listed = readers[
            jnp.clip(distance - 1, 0, readers.shape[0] - 1), jnp.maximum(source, 0)
        ]
        first = jnp.where(inside & (listed == 1), 0, 1 << 30)
        return kept(rows, rows, base, source * rows, jnp.maximum(begin, first))

    def add(block_ref, keep):
        for i in range(heads):
            at = pl.ds(i * rows, rows)
            weighted, sums = attend(
                query[at, :],
                block_ref[:, :head_dim],
                block_ref[:, head_dim:],
                keep,
                head_dim ** (-0.5),
            )
            num[at, :] += weighted
            den[at, :] += sums

    add(near, mask(chip - 2 + core))
    add(far, mask(chip - 1 - core))

    @pl.when(core == 1)
    def _():
        add(own, mask(block - 1))

    for i in range(heads):
        at = pl.ds(i * rows, rows)
        total = jnp.sum(den[at, :], axis=1, keepdims=True)
        gated[:, i * head_dim : (i + 1) * head_dim] = (num[at, :] / total * gate[at, :]).astype(BF16)
    count = 8
    piece = rows // count
    for i, step in enumerate(ORDER):
        source = lax.rem(head + jnp.where(core == 0, step, count - step), count)
        turned[i * piece : (i + 1) * piece, :] = gated[
            pl.ds(pl.multiple_of(source * piece, piece), piece), :
        ]
    parts[...] = jnp.dot(turned[...], ow[...], preferred_element_type=F32).astype(BF16)


ORDER = (2, 4, 6, 7, 1, 3, 5, 0)


def second_body(parts, got, a, b, c):
    piece = a.shape[0]
    for i, out in enumerate((a, b, c)):
        mine = parts[(4 + i) * piece : (5 + i) * piece, :].astype(F32)
        out[...] = (mine + got[i * piece : (i + 1) * piece, :].astype(F32)).astype(BF16)


def last_body(parts, a, b, c, d, out):
    piece = out.shape[0]
    total = parts[7 * piece :, :].astype(F32)
    for ref in (a, b, c, d):
        total = total + ref[...].astype(F32)
    out[...] = total.astype(BF16)


def shards(
    tokens,
    q_weight,
    gate_weight,
    k_weight,
    v_weight,
    q_gain,
    k_gain,
    out_weight,
    doc_starts,
    readers,
):
    rows, width = tokens.shape
    head_dim = q_gain.shape[0]
    heads = q_weight.shape[1] // head_dim
    kv_count = k_weight.shape[1] // head_dim
    kv_share = lax.axis_size("head") // kv_count
    seq, head = lax.axis_size("seq"), lax.axis_size("head")
    starts = doc_starts.reshape(1, -1)
    rope = jnp.asarray(rope_rows(head_dim))
    stacked = heads * rows

    def shape(r, c, dtype=BF16):
        return jax.ShapeDtypeStruct((r, c), dtype)

    own, trig = pl.pallas_call(
        functools.partial(kv_body, head_dim, kv_share),
        out_shape=(shape(rows, 2 * head_dim), shape(rows, 256, F32)),
        in_specs=[VMEM, VMEM, VMEM, ANY, ANY, ANY],
        out_specs=(VMEM, VMEM),
        scratch_shapes=[
            pltpu.VMEM((rows, width), BF16),
            pltpu.VMEM((width, head_dim), BF16),
            pltpu.VMEM((width, head_dim), BF16),
            pltpu.SemaphoreType.DMA((3,)),
        ],
        compiler_params=params(16),
        cost_estimate=cost(4 * rows * width * head_dim, 3 << 20),
        name="kv",
    )(starts, rope, k_gain.reshape(1, -1), tokens, k_weight, v_weight)

    near = lax.ppermute(own, "seq", [(i, (i + 2) % seq) for i in range(seq)])
    below = lax.ppermute(own, "seq", [(i, i ^ 1) for i in range(seq)])

    query, gate, num, den = pl.pallas_call(
        functools.partial(q_body, head_dim),
        out_shape=(
            shape(stacked, head_dim),
            shape(stacked, head_dim, F32),
            shape(stacked, head_dim, F32),
            shape(stacked, 128, F32),
        ),
        in_specs=[VMEM, VMEM, VMEM, VMEM, ANY, ANY, ANY],
        out_specs=(VMEM,) * 4,
        scratch_shapes=[
            pltpu.VMEM((rows, width), BF16),
            pltpu.VMEM((2 * heads, width, head_dim), BF16),
            pltpu.SemaphoreType.DMA((2 * heads + 1,)),
        ],
        compiler_params=params(20),
        cost_estimate=cost(4 * rows * width * heads * head_dim, 5 << 20),
        name="query",
    )(starts, q_gain.reshape(1, -1), trig, own, tokens, q_weight, gate_weight)

    far = lax.ppermute(near, "seq", [(i, i ^ 1) for i in range(seq)])

    parts = pl.pallas_call(
        functools.partial(out_body, head_dim),
        out_shape=shape(rows, width),
        in_specs=[VMEM, SMEM] + [VMEM] * 8,
        out_specs=VMEM,
        scratch_shapes=[
            pltpu.VMEM((rows, heads * head_dim), BF16),
            pltpu.VMEM((rows, heads * head_dim), BF16),
        ],
        compiler_params=params(20),
        cost_estimate=cost(2 * rows * width * heads * head_dim, 4 << 20),
        name="attend",
    )(starts, readers.T, query, gate, num, den, near, far, below, out_weight)

    def turn(block, step):
        route = []
        for s in range(seq):
            for h in range(head):
                to = (h + step) % head if s % 2 == 0 else (h - step) % head
                route.append((s * head + h, s * head + to))
        return lax.ppermute(block, ("seq", "head"), route)

    piece = rows // head
    got = turn(parts[: 3 * piece], 1)
    d = turn(parts[3 * piece : 4 * piece], -1)
    a, b, c = pl.pallas_call(
        second_body,
        out_shape=(shape(piece, width),) * 3,
        in_specs=[VMEM, VMEM],
        out_specs=(VMEM,) * 3,
        compiler_params=params(8),
        name="second",
    )(parts, got)
    b = turn(b, 3)
    c = turn(c, -3)
    a = turn(a, 1)
    return pl.pallas_call(
        last_body,
        out_shape=shape(piece, width),
        in_specs=[VMEM] * 5,
        out_specs=VMEM,
        compiler_params=params(8),
        name="last",
    )(parts, a, b, c, d)


def solution(mesh):
    placed = (
        P("seq", None),
        P(None, "head"),
        P(None, "head"),
        P(),
        P(),
        P(),
        P(),
        P("head", None),
        P(),
        P(),
    )
    return jax.shard_map(
        shards, mesh=mesh, in_specs=placed, out_specs=P(("seq", "head"), None), check_vma=False
    )
```

```python
import functools
import math

import jax
import jax.numpy as jnp
from jax import lax
from jax.experimental import pallas as pl
from jax.experimental.pallas import tpu as pltpu
from jax.sharding import PartitionSpec as P

HEADS = 16
ROPE_THETA = 10000000.0
EPSILON = 1e-06

F32 = jnp.float32
BF16 = jnp.bfloat16
HBM = pl.BlockSpec(memory_space=pltpu.HBM)
VMEM = pl.BlockSpec(memory_space=pltpu.VMEM)
SMEM = pl.BlockSpec(memory_space=pltpu.SMEM)


def params(mib):
    return pltpu.CompilerParams(vmem_limit_bytes=int(mib * (1 << 20)))


def cost(flops, nbytes, trans=0):
    return pl.CostEstimate(flops=flops, bytes_accessed=nbytes, transcendentals=trans)


def rope_angles(offset, head_dim):
    rot_width = head_dim // 4
    half = rot_width // 2
    lane = lax.broadcasted_iota(jnp.int32, (1, 128), 1)
    exponent = lax.rem(lane, half).astype(F32) * (-math.log(ROPE_THETA) * 2.0 / rot_width)
    frequency = jnp.where(lane < rot_width, jnp.exp(exponent), 0.0)
    angle = offset * frequency
    return jnp.cos(angle), jnp.sin(angle) * jnp.where(lane < half, -1.0, 1.0)


def doc_begin(starts, rows, base):
    at = base + lax.broadcasted_iota(jnp.int32, (rows, starts.shape[1]), 0)
    return jnp.max(jnp.where(starts <= at, starts, 0), axis=1, keepdims=True)


def normed_rotated(x, gain, cosine, sine, half):
    square = jnp.mean(x * x, axis=-1, keepdims=True)
    x = x * lax.rsqrt(square + EPSILON) * gain
    front = x[:, :128]
    lane = lax.broadcasted_iota(jnp.int32, front.shape, 1)
    partner = jnp.where(
        lane < half, pltpu.roll(front, 128 - half, 1), pltpu.roll(front, half, 1)
    )
    return front * cosine + partner * sine, x[:, 128:]


def kv_body(head_dim, kv_share, starts_in, gain_in, tok_in, kw_in, vw_in, kv, trig, starts, gain, tok, kw, vw, sems):
    rows = tok.shape[0]
    column = pl.multiple_of((lax.axis_index("head") // kv_share) * head_dim, head_dim)
    columns = pl.ds(column, head_dim)
    copies = [
        pltpu.make_async_copy(source, target, sems.at[i])
        for i, (source, target) in enumerate(
            (
                (starts_in, starts),
                (gain_in, gain),
                (tok_in, tok),
                (kw_in.at[:, columns], kw),
                (vw_in.at[:, columns], vw),
            )
        )
    ]
    for c in copies:
        c.start()
    base = lax.axis_index("seq") * rows
    copies[0].wait()
    begin = doc_begin(starts[...], rows, base)
    offset = (base + lax.broadcasted_iota(jnp.int32, (rows, 1), 0) - begin).astype(F32)
    cosine, sine = rope_angles(offset, head_dim)
    trig[:, :128] = cosine
    trig[:, 128:] = sine
    for c in copies[1:]:
        c.wait()
    key = jnp.dot(tok[...], kw[...], preferred_element_type=F32)
    kv[:, head_dim:] = jnp.dot(tok[...], vw[...], preferred_element_type=F32).astype(BF16)
    front, back = normed_rotated(key, gain[...], trig[:, :128], trig[:, 128:], head_dim // 8)
    kv[:, :128] = front.astype(BF16)
    kv[:, 128:head_dim] = back.astype(BF16)


def attend(query, key, value, keep, scale):
    scores = lax.dot_general(query, key, (((1,), (1,)), ((), ())), preferred_element_type=F32)
    weights = jnp.where(keep, jnp.exp(scores * scale), 0.0).astype(BF16)
    wide = weights.astype(F32)
    half = wide.shape[1] // 2
    return (
        jnp.dot(weights, value, preferred_element_type=F32),
        wide[:, :half] + wide[:, half:],
    )


def kept(rows, width, query_base, key_base, begin):
    at = query_base + lax.broadcasted_iota(jnp.int32, (rows, width), 0)
    key = key_base + lax.broadcasted_iota(jnp.int32, (rows, width), 1)
    return (key <= at) & (key >= begin)


def q_body(head_dim, starts_in, gain_in, trig, kv, tok_in, qw_in, gw_in, q_out, gate, num, den, starts, gain, tok, w, sems):
    rows = tok.shape[0]
    heads = qw_in.shape[1] // head_dim
    pairs = [(starts_in, starts), (gain_in, gain), (tok_in, tok)]
    small = len(pairs)
    for i in range(heads):
        columns = pl.ds(i * head_dim, head_dim)
        pairs.append((qw_in.at[:, columns], w.at[2 * i]))
        pairs.append((gw_in.at[:, columns], w.at[2 * i + 1]))
    copies = [
        pltpu.make_async_copy(source, target, sems.at[i])
        for i, (source, target) in enumerate(pairs)
    ]
    for c in copies:
        c.start()
    base = lax.axis_index("seq") * rows
    copies[0].wait()
    begin = doc_begin(starts[...], rows, base)
    keep = kept(rows, rows, base, base, begin)
    for c in copies[1:small]:
        c.wait()
    for i in range(heads):
        at = pl.ds(i * rows, rows)
        copies[small + 2 * i].wait()
        query = jnp.dot(tok[...], w[2 * i], preferred_element_type=F32)
        front, back = normed_rotated(query, gain[...], trig[:, :128], trig[:, 128:], head_dim // 8)
        q_out[at, :128] = front.astype(BF16)
        q_out[at, 128:] = back.astype(BF16)
        copies[small + 2 * i + 1].wait()
        logits = jnp.dot(tok[...], w[2 * i + 1], preferred_element_type=F32)
        gate[at, :] = 1.0 / (1.0 + jnp.exp(-logits))
        weighted, sums = attend(
            q_out[at, :], kv[:, :head_dim], kv[:, head_dim:], keep, head_dim ** (-0.5)
        )
        num[at, :] = weighted
        den[at, :] = sums


def out_body(head_dim, starts, readers, query, gate, num, den, near, far, own, ow, part_a, part_b, part_c, part_d, gated, turned):
    heads = query.shape[0] // head_dim
    rows = query.shape[0] // heads
    block = lax.axis_index("seq")
    core = lax.rem(block, 2)
    head = lax.axis_index("head")
    base = block * rows
    begin = doc_begin(starts[...], rows, base)
    chip = block - core

    def mask(source):
        distance = block - source
        inside = (source >= 0) & (distance >= 1) & (distance <= readers.shape[0])
        listed = readers[
            jnp.clip(distance - 1, 0, readers.shape[0] - 1), jnp.maximum(source, 0)
        ]
        first = jnp.where(inside & (listed == 1), 0, 1 << 30)
        return kept(rows, rows, base, source * rows, jnp.maximum(begin, first))

    def add(block_ref, keep):
        for i in range(heads):
            at = pl.ds(i * rows, rows)
            weighted, sums = attend(
                query[at, :],
                block_ref[:, :head_dim],
                block_ref[:, head_dim:],
                keep,
                head_dim ** (-0.5),
            )
            num[at, :] += weighted
            den[at, :] += sums

    add(near, mask(chip - 2 + core))
    add(far, mask(chip - 1 - core))

    @pl.when(core == 1)
    def _():
        add(own, mask(block - 1))

    for i in range(heads):
        at = pl.ds(i * rows, rows)
        total = jnp.sum(den[at, :], axis=1, keepdims=True)
        gated[:, i * head_dim : (i + 1) * head_dim] = (num[at, :] / total * gate[at, :]).astype(BF16)
    count = 8
    piece = rows // count
    for i, step in enumerate(ORDER):
        source = lax.rem(head + jnp.where(core == 0, step, count - step), count)
        turned[i * piece : (i + 1) * piece, :] = gated[
            pl.ds(pl.multiple_of(source * piece, piece), piece), :
        ]
    result = jnp.dot(turned[...], ow[...], preferred_element_type=F32).astype(BF16)
    at = 0
    for ref in (part_a, part_b, part_c, part_d):
        ref[...] = result[at : at + ref.shape[0], :]
        at += ref.shape[0]


ORDER = (1, 3, 7, 5, 4, 2, 6, 0)


def second_body(rest, got_a, got_b, got_c, forward, backward):
    piece = forward.shape[0]
    total = rest[:piece, :].astype(F32) + got_a[piece:, :].astype(F32) + got_c[...].astype(F32)
    forward[...] = total.astype(BF16)
    total = rest[piece : 2 * piece, :].astype(F32) + got_b[piece:, :].astype(F32)
    backward[...] = total.astype(BF16)


def last_body(rest, got_a, got_b, forward, backward, out):
    piece = out.shape[0]
    total = rest[2 * piece :, :].astype(F32)
    for ref in (got_a, got_b, forward, backward):
        total = total + ref[:piece, :].astype(F32)
    out[...] = total.astype(BF16)


def shards(
    tokens,
    q_weight,
    gate_weight,
    k_weight,
    v_weight,
    q_gain,
    k_gain,
    out_weight,
    doc_starts,
    readers,
):
    rows, width = tokens.shape
    head_dim = q_gain.shape[0]
    heads = q_weight.shape[1] // head_dim
    kv_count = k_weight.shape[1] // head_dim
    kv_share = lax.axis_size("head") // kv_count
    seq, head = lax.axis_size("seq"), lax.axis_size("head")
    starts = doc_starts.reshape(1, -1)
    stacked = heads * rows

    def shape(r, c, dtype=BF16):
        return jax.ShapeDtypeStruct((r, c), dtype)

    def held(r, c, dtype=BF16):
        return pltpu.VMEM((r, c), dtype)

    def far_away(*arrays):
        return tuple(pltpu.with_memory_space_constraint(x, pltpu.HBM) for x in arrays)

    own, trig = pl.pallas_call(
        functools.partial(kv_body, head_dim, kv_share),
        out_shape=(held(rows, 2 * head_dim), held(rows, 256, F32)),
        in_specs=[HBM] * 5,
        out_specs=(VMEM, VMEM),
        scratch_shapes=[
            pltpu.VMEM(starts.shape, jnp.int32),
            pltpu.VMEM((1, head_dim), F32),
            pltpu.VMEM((rows, width), BF16),
            pltpu.VMEM((width, head_dim), BF16),
            pltpu.VMEM((width, head_dim), BF16),
            pltpu.SemaphoreType.DMA((5,)),
        ],
        compiler_params=params(16),
        cost_estimate=cost(4 * rows * width * head_dim, 3 << 20),
        name="kv",
    )(*far_away(starts, k_gain.reshape(1, -1), tokens, k_weight, v_weight))

    near = lax.ppermute(own, "seq", [(i, i + 2) for i in range(seq - 2)])
    below = lax.ppermute(own, "seq", [(i, i ^ 1) for i in range(seq)])

    query, gate, num, den = pl.pallas_call(
        functools.partial(q_body, head_dim),
        out_shape=(
            held(stacked, head_dim),
            held(stacked, head_dim, F32),
            held(stacked, head_dim, F32),
            held(stacked, 128, F32),
        ),
        in_specs=[HBM] * 2 + [VMEM] * 2 + [HBM] * 3,
        out_specs=(VMEM,) * 4,
        scratch_shapes=[
            pltpu.VMEM(starts.shape, jnp.int32),
            pltpu.VMEM((1, head_dim), F32),
            pltpu.VMEM((rows, width), BF16),
            pltpu.VMEM((2 * heads, width, head_dim), BF16),
            pltpu.SemaphoreType.DMA((3 + 2 * heads,)),
        ],
        compiler_params=params(24),
        cost_estimate=cost(4 * rows * width * heads * head_dim, 5 << 20),
        name="query",
    )(*far_away(starts, q_gain.reshape(1, -1)), trig, own, *far_away(tokens, q_weight, gate_weight))

    near, query = lax.optimization_barrier((near, query))
    far = lax.ppermute(near, "seq", [(i, i ^ 1) for i in range(seq)])

    piece = rows // head
    part_a, part_b, part_c, rest = pl.pallas_call(
        functools.partial(out_body, head_dim),
        out_shape=tuple(shape(n * piece, width) for n in (2, 2, 1, 3)),
        in_specs=[VMEM, SMEM] + [VMEM] * 8,
        out_specs=(VMEM,) * 4,
        scratch_shapes=[
            pltpu.VMEM((rows, heads * head_dim), BF16),
            pltpu.VMEM((rows, heads * head_dim), BF16),
        ],
        compiler_params=params(20),
        cost_estimate=cost(2 * rows * width * heads * head_dim, 4 << 20),
        name="attend",
    )(starts, readers.T, query, gate, num, den, near, far, below, out_weight)

    def turn(block, step):
        route = []
        for s in range(seq):
            for h in range(head):
                to = (h + step) % head if s % 2 == 0 else (h - step) % head
                route.append((s * head + h, s * head + to))
        return lax.ppermute(block, ("seq", "head"), route)

    got_c = turn(part_c, 2)
    got_a = turn(part_a, 1)
    got_b = turn(part_b, -1)
    forward, backward = pl.pallas_call(
        second_body,
        out_shape=(shape(piece, width),) * 2,
        in_specs=[VMEM] * 4,
        out_specs=(VMEM,) * 2,
        compiler_params=params(8),
        name="second",
    )(rest, got_a, got_b, got_c)
    forward = turn(forward, 2)
    backward = turn(backward, -2)
    return pl.pallas_call(
        last_body,
        out_shape=shape(piece, width),
        in_specs=[VMEM] * 5,
        out_specs=VMEM,
        compiler_params=params(8),
        name="last",
    )(rest, got_a, got_b, forward, backward)


def solution(mesh):
    placed = (
        P("seq", None),
        P(None, "head"),
        P(None, "head"),
        P(),
        P(),
        P(),
        P(),
        P("head", None),
        P(),
        P(),
    )
    return jax.shard_map(
        shards, mesh=mesh, in_specs=placed, out_specs=P(("seq", "head"), None), check_vma=False
    )
```

```python
import functools
import math

import jax
import jax.numpy as jnp
from jax import lax
from jax.experimental import pallas as pl
from jax.experimental.pallas import tpu as pltpu
from jax.sharding import PartitionSpec as P


ROPE_THETA = 10000000.0
EPSILON = 1e-06

F32 = jnp.float32
BF16 = jnp.bfloat16
HBM = pl.BlockSpec(memory_space=pltpu.HBM)
VMEM = pl.BlockSpec(memory_space=pltpu.VMEM)
SMEM = pl.BlockSpec(memory_space=pltpu.SMEM)


def params(mib):
    return pltpu.CompilerParams(vmem_limit_bytes=int(mib * (1 << 20)))


def cost(flops, nbytes, trans=0):
    return pl.CostEstimate(flops=flops, bytes_accessed=nbytes, transcendentals=trans)


def rope_angles(offset, head_dim):
    rot_width = head_dim // 4
    half = rot_width // 2
    lane = lax.broadcasted_iota(jnp.int32, (1, 128), 1)
    exponent = lax.rem(lane, half).astype(F32) * (-math.log(ROPE_THETA) * 2.0 / rot_width)
    frequency = jnp.where(lane < rot_width, jnp.exp(exponent), 0.0)
    angle = offset * frequency
    return jnp.cos(angle), jnp.sin(angle) * jnp.where(lane < half, -1.0, 1.0)


def doc_begin(starts, rows, base):
    at = base + lax.broadcasted_iota(jnp.int32, (rows, starts.shape[1]), 0)
    return jnp.max(jnp.where(starts <= at, starts, 0), axis=1, keepdims=True)


def normed_rotated(x, gain, cosine, sine, half):
    square = jnp.mean(x * x, axis=-1, keepdims=True)
    x = x * lax.rsqrt(square + EPSILON) * gain
    front = x[:, :128]
    lane = lax.broadcasted_iota(jnp.int32, front.shape, 1)
    partner = jnp.where(
        lane < half, pltpu.roll(front, 128 - half, 1), pltpu.roll(front, half, 1)
    )
    return front * cosine + partner * sine, x[:, 128:]


def kv_body(head_dim, kv_share, starts_in, gain_in, tok_in, kw_in, vw_in, qw_in, gw_in, kv, trig, tok, qw, gw, starts, gain, kw, vw, sems):
    rows = tok.shape[0]
    column = pl.multiple_of((lax.axis_index("head") // kv_share) * head_dim, head_dim)
    columns = pl.ds(column, head_dim)
    copies = [
        pltpu.make_async_copy(source, target, sems.at[i])
        for i, (source, target) in enumerate(
            (
                (starts_in, starts),
                (gain_in, gain),
                (tok_in, tok),
                (kw_in.at[:, columns], kw),
                (vw_in.at[:, columns], vw),
                (qw_in, qw),
                (gw_in, gw),
            )
        )
    ]
    for c in copies:
        c.start()
    base = lax.axis_index("seq") * rows
    copies[0].wait()
    begin = doc_begin(starts[...], rows, base)
    offset = (base + lax.broadcasted_iota(jnp.int32, (rows, 1), 0) - begin).astype(F32)
    cosine, sine = rope_angles(offset, head_dim)
    trig[:, :128] = cosine
    trig[:, 128:] = sine
    for c in copies[1:5]:
        c.wait()
    key = jnp.dot(tok[...], kw[...], preferred_element_type=F32)
    kv[:, head_dim:] = jnp.dot(tok[...], vw[...], preferred_element_type=F32).astype(BF16)
    front, back = normed_rotated(key, gain[...], trig[:, :128], trig[:, 128:], head_dim // 8)
    kv[:, :128] = front.astype(BF16)
    kv[:, 128:head_dim] = back.astype(BF16)
    for c in copies[5:]:
        c.wait()


def attend(query, key, value, keep, scale):
    scores = lax.dot_general(query, key, (((1,), (1,)), ((), ())), preferred_element_type=F32)
    weights = jnp.where(keep, jnp.exp(scores * scale), 0.0).astype(BF16)
    wide = weights.astype(F32)
    half = wide.shape[1] // 2
    return (
        jnp.dot(weights, value, preferred_element_type=F32),
        wide[:, :half] + wide[:, half:],
    )


def kept(rows, width, query_base, key_base, begin):
    at = query_base + lax.broadcasted_iota(jnp.int32, (rows, width), 0)
    key = key_base + lax.broadcasted_iota(jnp.int32, (rows, width), 1)
    return (key <= at) & (key >= begin)


def q_body(head_dim, starts, gain, trig, kv, tok, qw, gw, q_out, gate, num, den):
    rows = tok.shape[0]
    heads = qw.shape[1] // head_dim
    base = lax.axis_index("seq") * rows
    begin = doc_begin(starts[...], rows, base)
    keep = kept(rows, rows, base, base, begin)
    for i in range(heads):
        at = pl.ds(i * rows, rows)
        columns = slice(i * head_dim, (i + 1) * head_dim)
        query = jnp.dot(tok[...], qw[:, columns], preferred_element_type=F32)
        front, back = normed_rotated(query, gain[...], trig[:, :128], trig[:, 128:], head_dim // 8)
        q_out[at, :128] = front.astype(BF16)
        q_out[at, 128:] = back.astype(BF16)
        logits = jnp.dot(tok[...], gw[:, columns], preferred_element_type=F32)
        gate[at, :] = 1.0 / (1.0 + jnp.exp(-logits))
        weighted, sums = attend(
            q_out[at, :], kv[:, :head_dim], kv[:, head_dim:], keep, head_dim ** (-0.5)
        )
        num[at, :] = weighted
        den[at, :] = sums


def source_mask(starts, readers, rows, source):
    block = lax.axis_index("seq")
    span = readers.shape[0]
    distance = block - source
    inside = (source >= 0) & (distance >= 1) & (distance <= span)
    listed = readers[jnp.clip(distance - 1, 0, span - 1), jnp.maximum(source, 0)]
    first = jnp.where(inside & (listed == 1), 0, 1 << 30)
    begin = doc_begin(starts[...], rows, block * rows)
    return kept(rows, rows, block * rows, source * rows, jnp.maximum(begin, first))


def attend_block(head_dim, query, block, keep, num_in, den_in, num, den):
    rows = keep.shape[0]
    for i in range(query.shape[0] // rows):
        at = pl.ds(i * rows, rows)
        weighted, sums = attend(
            query[at, :], block[:, :head_dim], block[:, head_dim:], keep, head_dim ** (-0.5)
        )
        num[at, :] = num_in[at, :] + weighted
        den[at, :] = den_in[at, :] + sums


def near_body(head_dim, starts, readers, query, num_in, den_in, near, own, num, den):
    rows = near.shape[0]
    block = lax.axis_index("seq")
    core = lax.rem(block, 2)
    keep = source_mask(starts, readers, rows, block - 2)
    attend_block(head_dim, query, near, keep, num_in, den_in, num, den)

    @pl.when(core == 1)
    def _():
        keep = source_mask(starts, readers, rows, block - 1)
        attend_block(head_dim, query, own, keep, num, den, num, den)


def out_body(head_dim, starts, readers, query, gate, num_in, den_in, far, ow, part_a, part_b, part_c, part_d, num, den, gated, turned):
    rows = far.shape[0]
    heads = query.shape[0] // rows
    block = lax.axis_index("seq")
    core = lax.rem(block, 2)
    head = lax.axis_index("head")
    keep = source_mask(starts, readers, rows, block - 1 - 2 * core)
    attend_block(head_dim, query, far, keep, num_in, den_in, num, den)
    for i in range(heads):
        at = pl.ds(i * rows, rows)
        total = jnp.sum(den[at, :], axis=1, keepdims=True)
        gated[:, i * head_dim : (i + 1) * head_dim] = (num[at, :] / total * gate[at, :]).astype(BF16)
    count = 8
    piece = rows // count
    for i, step in enumerate(ORDER):
        source = lax.rem(head + jnp.where(core == 0, step, count - step), count)
        turned[i * piece : (i + 1) * piece, :] = gated[
            pl.ds(pl.multiple_of(source * piece, piece), piece), :
        ]
    result = jnp.dot(turned[...], ow[...], preferred_element_type=F32).astype(BF16)
    at = 0
    for ref in (part_a, part_b, part_c, part_d):
        ref[...] = result[at : at + ref.shape[0], :]
        at += ref.shape[0]


ORDER = (1, 3, 7, 5, 4, 2, 6, 0)


def forward_body(rest, got_a, got_c, out):
    piece = out.shape[0]
    total = rest[:piece, :].astype(F32) + got_a[piece:, :].astype(F32) + got_c[...].astype(F32)
    out[...] = total.astype(BF16)


def backward_body(rest, got_b, out):
    piece = out.shape[0]
    total = rest[piece : 2 * piece, :].astype(F32) + got_b[piece:, :].astype(F32)
    out[...] = total.astype(BF16)


def last_body(rest, got_a, got_b, forward, backward, out):
    piece = out.shape[0]
    total = rest[2 * piece :, :].astype(F32)
    for ref in (got_a, got_b, forward, backward):
        total = total + ref[:piece, :].astype(F32)
    out[...] = total.astype(BF16)


def shards(
    tokens,
    q_weight,
    gate_weight,
    k_weight,
    v_weight,
    q_gain,
    k_gain,
    out_weight,
    doc_starts,
    readers,
):
    rows, width = tokens.shape
    head_dim = q_gain.shape[0]
    heads = q_weight.shape[1] // head_dim
    kv_count = k_weight.shape[1] // head_dim
    kv_share = lax.axis_size("head") // kv_count
    seq, head = lax.axis_size("seq"), lax.axis_size("head")
    starts = doc_starts.reshape(1, -1)
    stacked = heads * rows

    def shape(r, c, dtype=BF16):
        return jax.ShapeDtypeStruct((r, c), dtype)

    def held(r, c, dtype=BF16):
        return pltpu.VMEM((r, c), dtype)

    def far_away(*arrays):
        return tuple(pltpu.with_memory_space_constraint(x, pltpu.HBM) for x in arrays)

    own, trig, near_tokens, near_q, near_gate = pl.pallas_call(
        functools.partial(kv_body, head_dim, kv_share),
        out_shape=(
            held(rows, 2 * head_dim),
            held(rows, 256, F32),
            held(rows, width),
            held(*q_weight.shape),
            held(*gate_weight.shape),
        ),
        in_specs=[HBM] * 7,
        out_specs=(VMEM,) * 5,
        scratch_shapes=[
            pltpu.VMEM(starts.shape, jnp.int32),
            pltpu.VMEM((1, head_dim), F32),
            pltpu.VMEM((width, head_dim), BF16),
            pltpu.VMEM((width, head_dim), BF16),
            pltpu.SemaphoreType.DMA((7,)),
        ],
        compiler_params=params(16),
        cost_estimate=cost(4 * rows * width * head_dim, 7 << 20),
        name="kv",
    )(
        *far_away(
            starts, k_gain.reshape(1, -1), tokens, k_weight, v_weight, q_weight, gate_weight
        )
    )

    near = lax.ppermute(own, "seq", [(i, i + 2) for i in range(seq - 2)])
    below = lax.ppermute(own, "seq", [(i, i ^ 1) for i in range(seq)])

    query, gate, num, den = pl.pallas_call(
        functools.partial(q_body, head_dim),
        out_shape=(
            held(stacked, head_dim),
            held(stacked, head_dim, F32),
            held(stacked, head_dim, F32),
            held(stacked, 128, F32),
        ),
        in_specs=[VMEM] * 7,
        out_specs=(VMEM,) * 4,
        compiler_params=params(24),
        cost_estimate=cost(4 * rows * width * heads * head_dim, 5 << 20),
        name="query",
    )(starts, q_gain.reshape(1, -1), trig, own, near_tokens, near_q, near_gate)

    near, query = lax.optimization_barrier((near, query))
    far = lax.ppermute(near, "seq", [(i, i ^ 1) for i in range(seq)])

    table = readers.T
    num, den = pl.pallas_call(
        functools.partial(near_body, head_dim),
        out_shape=(held(stacked, head_dim, F32), held(stacked, 128, F32)),
        in_specs=[VMEM, SMEM] + [VMEM] * 5,
        out_specs=(VMEM,) * 2,
        compiler_params=params(16),
        cost_estimate=cost(4 * stacked * rows * head_dim, 3 << 20),
        name="near",
    )(starts, table, query, num, den, near, below)

    piece = rows // head
    part_a, part_b, part_c, rest = pl.pallas_call(
        functools.partial(out_body, head_dim),
        out_shape=tuple(held(n * piece, width) for n in (2, 2, 1, 3)),
        in_specs=[VMEM, SMEM] + [VMEM] * 6,
        out_specs=(VMEM,) * 4,
        scratch_shapes=[
            pltpu.VMEM((stacked, head_dim), F32),
            pltpu.VMEM((stacked, 128), F32),
            pltpu.VMEM((rows, heads * head_dim), BF16),
            pltpu.VMEM((rows, heads * head_dim), BF16),
        ],
        compiler_params=params(24),
        cost_estimate=cost(2 * rows * width * heads * head_dim, 4 << 20),
        name="attend",
    )(starts, table, query, gate, num, den, far, out_weight)

    def turn(block, step):
        route = []
        for s in range(seq):
            for h in range(head):
                to = (h + step) % head if s % 2 == 0 else (h - step) % head
                route.append((s * head + h, s * head + to))
        return lax.ppermute(block, ("seq", "head"), route)

    def summed(body, *blocks):
        return pl.pallas_call(
            body,
            out_shape=held(piece, width),
            in_specs=[VMEM] * len(blocks),
            out_specs=VMEM,
            compiler_params=params(8),
            cost_estimate=cost(4 * piece * width, 8 * piece * width),
        )(*blocks)

    got_a = turn(part_a, 1)
    got_c = turn(part_c, 2)
    got_b = turn(part_b, -1)
    forward = turn(summed(forward_body, rest, got_a, got_c), 2)
    backward = turn(summed(backward_body, rest, got_b), -2)
    return pl.pallas_call(
        last_body,
        out_shape=shape(piece, width),
        in_specs=[VMEM] * 5,
        out_specs=VMEM,
        compiler_params=params(8),
        name="last",
    )(rest, got_a, got_b, forward, backward)


def solution(mesh):
    placed = (
        P("seq", None),
        P(None, "head"),
        P(None, "head"),
        P(),
        P(),
        P(),
        P(),
        P("head", None),
        P(),
        P(),
    )
    return jax.shard_map(
        shards, mesh=mesh, in_specs=placed, out_specs=P(("seq", "head"), None), check_vma=False
    )
```

```python
import functools
import math

import jax
import jax.numpy as jnp
from jax import lax
from jax.experimental import pallas as pl
from jax.experimental.pallas import tpu as pltpu
from jax.sharding import PartitionSpec as P


ROPE_THETA = 10000000.0
EPSILON = 1e-06

F32 = jnp.float32
BF16 = jnp.bfloat16
HBM = pl.BlockSpec(memory_space=pltpu.HBM)
VMEM = pl.BlockSpec(memory_space=pltpu.VMEM)
SMEM = pl.BlockSpec(memory_space=pltpu.SMEM)


def params(mib):
    return pltpu.CompilerParams(vmem_limit_bytes=int(mib * (1 << 20)))


def cost(flops, nbytes, trans=0):
    return pl.CostEstimate(flops=flops, bytes_accessed=nbytes, transcendentals=trans)


def rope_angles(offset, head_dim):
    rot_width = head_dim // 4
    half = rot_width // 2
    lane = lax.broadcasted_iota(jnp.int32, (1, 128), 1)
    exponent = lax.rem(lane, half).astype(F32) * (-math.log(ROPE_THETA) * 2.0 / rot_width)
    frequency = jnp.where(lane < rot_width, jnp.exp(exponent), 0.0)
    angle = offset * frequency
    return jnp.cos(angle), jnp.sin(angle) * jnp.where(lane < half, -1.0, 1.0)


def doc_begin(starts, rows, base):
    at = base + lax.broadcasted_iota(jnp.int32, (rows, starts.shape[1]), 0)
    return jnp.max(jnp.where(starts <= at, starts, 0), axis=1, keepdims=True)


def normed_rotated(x, gain, cosine, sine, half):
    square = jnp.mean(x * x, axis=-1, keepdims=True)
    x = x * lax.rsqrt(square + EPSILON) * gain
    front = x[:, :128]
    lane = lax.broadcasted_iota(jnp.int32, front.shape, 1)
    partner = jnp.where(
        lane < half, pltpu.roll(front, 128 - half, 1), pltpu.roll(front, half, 1)
    )
    return front * cosine + partner * sine, x[:, 128:]


def kv_body(head_dim, kv_share, starts_in, gain_in, tok_in, kw_in, vw_in, qw_in, gw_in, kv, trig, tok, qw, gw, starts, gain, kw, vw, sems):
    rows = tok.shape[0]
    column = pl.multiple_of((lax.axis_index("head") // kv_share) * head_dim, head_dim)
    columns = pl.ds(column, head_dim)
    half = tok.shape[1] // 2
    low, high = pl.ds(0, half), pl.ds(half, half)
    pairs = (
        (starts_in, starts),
        (gain_in, gain),
        (tok_in.at[:, low], tok.at[:, low]),
        (kw_in.at[low, columns], kw.at[low, :]),
        (tok_in.at[:, high], tok.at[:, high]),
        (kw_in.at[high, columns], kw.at[high, :]),
        (vw_in.at[:, columns], vw),
        (qw_in, qw),
        (gw_in, gw),
    )
    copies = [pltpu.make_async_copy(a, b, sems.at[i]) for i, (a, b) in enumerate(pairs)]
    for c in copies[:7]:
        c.start()
    base = lax.axis_index("seq") * rows
    copies[0].wait()
    begin = doc_begin(starts[...], rows, base)
    offset = (base + lax.broadcasted_iota(jnp.int32, (rows, 1), 0) - begin).astype(F32)
    cosine, sine = rope_angles(offset, head_dim)
    trig[:, :128] = cosine
    trig[:, 128:] = sine
    for c in copies[1:4]:
        c.wait()
    key = jnp.dot(tok[:, :half], kw[:half, :], preferred_element_type=F32)
    for c in copies[4:6]:
        c.wait()
    for c in copies[7:]:
        c.start()
    key = key + jnp.dot(tok[:, half:], kw[half:, :], preferred_element_type=F32)
    copies[6].wait()
    kv[:, head_dim:] = jnp.dot(tok[...], vw[...], preferred_element_type=F32).astype(BF16)
    front, back = normed_rotated(key, gain[...], trig[:, :128], trig[:, 128:], head_dim // 8)
    kv[:, :128] = front.astype(BF16)
    kv[:, 128:head_dim] = back.astype(BF16)
    for c in copies[7:]:
        c.wait()


def attend(query, key, value, keep, scale):
    scores = lax.dot_general(query, key, (((1,), (1,)), ((), ())), preferred_element_type=F32)
    weights = jnp.where(keep, jnp.exp(scores * scale), 0.0).astype(BF16)
    wide = weights.astype(F32)
    half = wide.shape[1] // 2
    return (
        jnp.dot(weights, value, preferred_element_type=F32),
        wide[:, :half] + wide[:, half:],
    )


def kept(rows, width, query_base, key_base, begin):
    at = query_base + lax.broadcasted_iota(jnp.int32, (rows, width), 0)
    key = key_base + lax.broadcasted_iota(jnp.int32, (rows, width), 1)
    return (key <= at) & (key >= begin)


def q_body(head_dim, starts, gain, trig, kv, tok, qw, gw, q_out, gate, num, den):
    rows = tok.shape[0]
    heads = qw.shape[1] // head_dim
    base = lax.axis_index("seq") * rows
    begin = doc_begin(starts[...], rows, base)
    keep = kept(rows, rows, base, base, begin)
    for i in range(heads):
        at = pl.ds(i * rows, rows)
        columns = slice(i * head_dim, (i + 1) * head_dim)
        query = jnp.dot(tok[...], qw[:, columns], preferred_element_type=F32)
        front, back = normed_rotated(query, gain[...], trig[:, :128], trig[:, 128:], head_dim // 8)
        q_out[at, :128] = front.astype(BF16)
        q_out[at, 128:] = back.astype(BF16)
        logits = jnp.dot(tok[...], gw[:, columns], preferred_element_type=F32)
        gate[at, :] = 1.0 / (1.0 + jnp.exp(-logits))
        weighted, sums = attend(
            q_out[at, :], kv[:, :head_dim], kv[:, head_dim:], keep, head_dim ** (-0.5)
        )
        num[at, :] = weighted
        den[at, :] = sums


def source_mask(starts, readers, rows, source):
    block = lax.axis_index("seq")
    span = readers.shape[0]
    distance = block - source
    inside = (source >= 0) & (distance >= 1) & (distance <= span)
    listed = readers[jnp.clip(distance - 1, 0, span - 1), jnp.maximum(source, 0)]
    first = jnp.where(inside & (listed == 1), 0, 1 << 30)
    begin = doc_begin(starts[...], rows, block * rows)
    return kept(rows, rows, block * rows, source * rows, jnp.maximum(begin, first))


def attend_block(head_dim, query, block, keep, num_in, den_in, num, den):
    rows = keep.shape[0]
    for i in range(query.shape[0] // rows):
        at = pl.ds(i * rows, rows)
        weighted, sums = attend(
            query[at, :], block[:, :head_dim], block[:, head_dim:], keep, head_dim ** (-0.5)
        )
        num[at, :] = num_in[at, :] + weighted
        den[at, :] = den_in[at, :] + sums


def near_body(head_dim, starts, readers, query, num_in, den_in, near, own, num, den):
    rows = near.shape[0]
    block = lax.axis_index("seq")
    core = lax.rem(block, 2)
    keep = source_mask(starts, readers, rows, block - 2)
    attend_block(head_dim, query, near, keep, num_in, den_in, num, den)

    @pl.when(core == 1)
    def _():
        keep = source_mask(starts, readers, rows, block - 1)
        attend_block(head_dim, query, own, keep, num, den, num, den)


def out_body(head_dim, starts, readers, query, gate, num_in, den_in, far, ow, part_a, part_b, part_c, part_d, num, den, gated, turned):
    rows = far.shape[0]
    heads = query.shape[0] // rows
    block = lax.axis_index("seq")
    core = lax.rem(block, 2)
    head = lax.axis_index("head")
    keep = source_mask(starts, readers, rows, block - 1 - 2 * core)
    attend_block(head_dim, query, far, keep, num_in, den_in, num, den)
    for i in range(heads):
        at = pl.ds(i * rows, rows)
        total = jnp.sum(den[at, :], axis=1, keepdims=True)
        gated[:, i * head_dim : (i + 1) * head_dim] = (num[at, :] / total * gate[at, :]).astype(BF16)
    count = 8
    piece = rows // count
    for i, step in enumerate(ORDER):
        source = lax.rem(head + jnp.where(lax.rem(head + core, 2) == 0, step, count - step), count)
        turned[i * piece : (i + 1) * piece, :] = gated[
            pl.ds(pl.multiple_of(source * piece, piece), piece), :
        ]
    result = jnp.dot(turned[...], ow[...], preferred_element_type=F32).astype(BF16)
    at = 0
    for ref in (part_a, part_b, part_c, part_d):
        ref[...] = result[at : at + ref.shape[0], :]
        at += ref.shape[0]


ORDER = (1, 3, 7, 5, 4, 6, 2, 0)


def first_body(rest, got_a, got_c, out):
    piece = out.shape[0]
    total = rest[:piece, :].astype(F32) + got_a[piece:, :].astype(F32) + got_c[...].astype(F32)
    out[...] = total.astype(BF16)


def second_body(rest, got_b, out):
    piece = out.shape[0]
    total = rest[piece : 2 * piece, :].astype(F32) + got_b[piece:, :].astype(F32)
    out[...] = total.astype(BF16)


def last_body(rest, got_a, got_b, first, second, out):
    piece = out.shape[0]
    total = rest[2 * piece :, :].astype(F32)
    for ref in (got_a, got_b, first, second):
        total = total + ref[:piece, :].astype(F32)
    out[...] = total.astype(BF16)


def shards(
    tokens,
    q_weight,
    gate_weight,
    k_weight,
    v_weight,
    q_gain,
    k_gain,
    out_weight,
    doc_starts,
    readers,
):
    rows, width = tokens.shape
    head_dim = q_gain.shape[0]
    heads = q_weight.shape[1] // head_dim
    kv_count = k_weight.shape[1] // head_dim
    kv_share = lax.axis_size("head") // kv_count
    seq, head = lax.axis_size("seq"), lax.axis_size("head")
    starts = doc_starts.reshape(1, -1)
    stacked = heads * rows

    def shape(r, c, dtype=BF16):
        return jax.ShapeDtypeStruct((r, c), dtype)

    def held(r, c, dtype=BF16):
        return pltpu.VMEM((r, c), dtype)

    def far_away(*arrays):
        return tuple(pltpu.with_memory_space_constraint(x, pltpu.HBM) for x in arrays)

    own, trig, near_tokens, near_q, near_gate = pl.pallas_call(
        functools.partial(kv_body, head_dim, kv_share),
        out_shape=(
            held(rows, 2 * head_dim),
            held(rows, 256, F32),
            held(rows, width),
            held(*q_weight.shape),
            held(*gate_weight.shape),
        ),
        in_specs=[HBM] * 7,
        out_specs=(VMEM,) * 5,
        scratch_shapes=[
            pltpu.VMEM(starts.shape, jnp.int32),
            pltpu.VMEM((1, head_dim), F32),
            pltpu.VMEM((width, head_dim), BF16),
            pltpu.VMEM((width, head_dim), BF16),
            pltpu.SemaphoreType.DMA((9,)),
        ],
        compiler_params=params(16),
        cost_estimate=cost(4 * rows * width * head_dim, 7 << 20),
        name="kv",
    )(
        *far_away(
            starts, k_gain.reshape(1, -1), tokens, k_weight, v_weight, q_weight, gate_weight
        )
    )

    near = lax.ppermute(own, "seq", [(i, i + 2) for i in range(seq - 2)])
    below = lax.ppermute(own, "seq", [(i, i ^ 1) for i in range(seq)])

    query, gate, num, den = pl.pallas_call(
        functools.partial(q_body, head_dim),
        out_shape=(
            held(stacked, head_dim),
            held(stacked, head_dim, F32),
            held(stacked, head_dim, F32),
            held(stacked, 128, F32),
        ),
        in_specs=[VMEM] * 7,
        out_specs=(VMEM,) * 4,
        compiler_params=params(24),
        cost_estimate=cost(4 * rows * width * heads * head_dim, 5 << 20),
        name="query",
    )(starts, q_gain.reshape(1, -1), trig, own, near_tokens, near_q, near_gate)

    near, query = lax.optimization_barrier((near, query))
    far = lax.ppermute(near, "seq", [(i, i ^ 1) for i in range(seq)])

    table = readers.T
    num, den = pl.pallas_call(
        functools.partial(near_body, head_dim),
        out_shape=(held(stacked, head_dim, F32), held(stacked, 128, F32)),
        in_specs=[VMEM, SMEM] + [VMEM] * 5,
        out_specs=(VMEM,) * 2,
        compiler_params=params(16),
        cost_estimate=cost(4 * stacked * rows * head_dim, 3 << 20),
        name="near",
    )(starts, table, query, num, den, near, below)

    piece = rows // head
    part_a, part_b, part_c, rest = pl.pallas_call(
        functools.partial(out_body, head_dim),
        out_shape=tuple(held(n * piece, width) for n in (2, 2, 1, 3)),
        in_specs=[VMEM, SMEM] + [VMEM] * 6,
        out_specs=(VMEM,) * 4,
        scratch_shapes=[
            pltpu.VMEM((stacked, head_dim), F32),
            pltpu.VMEM((stacked, 128), F32),
            pltpu.VMEM((rows, heads * head_dim), BF16),
            pltpu.VMEM((rows, heads * head_dim), BF16),
        ],
        compiler_params=params(24),
        cost_estimate=cost(2 * rows * width * heads * head_dim, 4 << 20),
        name="attend",
    )(starts, table, query, gate, num, den, far, out_weight)

    def turn(block, step):
        route = []
        for s in range(seq):
            for h in range(head):
                to = (h + step) % head if (s + h) % 2 == 0 else (h - step) % head
                route.append((s * head + h, s * head + to))
        return lax.ppermute(block, ("seq", "head"), route)

    def summed(body, *blocks):
        return pl.pallas_call(
            body,
            out_shape=held(piece, width),
            in_specs=[VMEM] * len(blocks),
            out_specs=VMEM,
            compiler_params=params(8),
            cost_estimate=cost(4 * piece * width, 8 * piece * width),
        )(*blocks)

    got_a = turn(part_a, 1)
    got_c = turn(part_c, -2)
    got_b = turn(part_b, -1)
    first = turn(summed(first_body, rest, got_a, got_c), -2)
    second = turn(summed(second_body, rest, got_b), 2)
    return pl.pallas_call(
        last_body,
        out_shape=shape(piece, width),
        in_specs=[VMEM] * 5,
        out_specs=VMEM,
        compiler_params=params(8),
        name="last",
    )(rest, got_a, got_b, first, second)


def solution(mesh):
    placed = (
        P("seq", None),
        P(None, "head"),
        P(None, "head"),
        P(),
        P(),
        P(),
        P(),
        P("head", None),
        P(),
        P(),
    )
    return jax.shard_map(
        shards, mesh=mesh, in_specs=placed, out_specs=P(("seq", "head"), None), check_vma=False
    )
```

```python
import functools
import math

import jax
import jax.numpy as jnp
from jax import lax
from jax.experimental import pallas as pl
from jax.experimental.pallas import tpu as pltpu
from jax.sharding import PartitionSpec as P


ROPE_THETA = 10000000.0
EPSILON = 1e-06

F32 = jnp.float32
BF16 = jnp.bfloat16
HBM = pl.BlockSpec(memory_space=pltpu.HBM)
VMEM = pl.BlockSpec(memory_space=pltpu.VMEM)
SMEM = pl.BlockSpec(memory_space=pltpu.SMEM)


def params(mib):
    return pltpu.CompilerParams(vmem_limit_bytes=int(mib * (1 << 20)))


def cost(flops, nbytes, trans=0):
    return pl.CostEstimate(flops=flops, bytes_accessed=nbytes, transcendentals=trans)


def rope_angles(offset, head_dim):
    rot_width = head_dim // 4
    half = rot_width // 2
    lane = lax.broadcasted_iota(jnp.int32, (1, 128), 1)
    exponent = lax.rem(lane, half).astype(F32) * (-math.log(ROPE_THETA) * 2.0 / rot_width)
    frequency = jnp.where(lane < rot_width, jnp.exp(exponent), 0.0)
    angle = offset * frequency
    return jnp.cos(angle), jnp.sin(angle) * jnp.where(lane < half, -1.0, 1.0)


def rows_from(base, rows):
    return base + lax.broadcasted_iota(jnp.int32, (rows, 1), 0)


def doc_begin(starts, at):
    return jnp.max(jnp.where(starts <= at, starts, 0), axis=1, keepdims=True)


def normed_rotated(x, gain, cosine, sine, half):
    square = jnp.mean(x * x, axis=-1, keepdims=True)
    x = x * lax.rsqrt(square + EPSILON) * gain
    front = x[:, :128]
    lane = lax.broadcasted_iota(jnp.int32, front.shape, 1)
    partner = jnp.where(
        lane < half, pltpu.roll(front, 128 - half, 1), pltpu.roll(front, half, 1)
    )
    return front * cosine + partner * sine, x[:, 128:]


def kv_body(head_dim, kv_share, starts_in, gain_in, tok_in, kw_in, vw_in, qw_in, kv, trig, tok, qw, starts, gain, kw, vw, sems):
    rows = tok.shape[0]
    column = pl.multiple_of((lax.axis_index("head") // kv_share) * head_dim, head_dim)
    columns = pl.ds(column, head_dim)
    half = tok.shape[1] // 2
    low, high = pl.ds(0, half), pl.ds(half, half)
    pairs = (
        (starts_in, starts),
        (gain_in, gain),
        (tok_in.at[:, low], tok.at[:, low]),
        (kw_in.at[low, columns], kw.at[low, :]),
        (tok_in.at[:, high], tok.at[:, high]),
        (kw_in.at[high, columns], kw.at[high, :]),
        (vw_in.at[:, columns], vw),
        (qw_in, qw),
    )
    copies = [pltpu.make_async_copy(a, b, sems.at[i]) for i, (a, b) in enumerate(pairs)]
    for c in copies:
        c.start()
    base = lax.axis_index("seq") * rows
    copies[0].wait()
    at = rows_from(base, rows)
    offset = (at - doc_begin(starts[...], at)).astype(F32)
    cosine, sine = rope_angles(offset, head_dim)
    trig[:, :128] = cosine
    trig[:, 128:] = sine
    for c in copies[1:4]:
        c.wait()
    key = jnp.dot(tok[:, :half], kw[:half, :], preferred_element_type=F32)
    for c in copies[4:6]:
        c.wait()
    key = key + jnp.dot(tok[:, half:], kw[half:, :], preferred_element_type=F32)
    copies[6].wait()
    kv[:, head_dim:] = jnp.dot(tok[...], vw[...], preferred_element_type=F32).astype(BF16)
    front, back = normed_rotated(key, gain[...], trig[:, :128], trig[:, 128:], head_dim // 8)
    kv[:, :128] = front.astype(BF16)
    kv[:, 128:head_dim] = back.astype(BF16)
    copies[7].wait()


def attend(query, key, value, keep, scale):
    scores = lax.dot_general(query, key, (((1,), (1,)), ((), ())), preferred_element_type=F32)
    rows = keep.shape[0]
    weights = jnp.concatenate(
        [
            jnp.where(keep, jnp.exp(scores[i : i + rows] * scale), 0.0)
            for i in range(0, query.shape[0], rows)
        ]
    ).astype(BF16)
    wide = weights.astype(F32)
    half = wide.shape[1] // 2
    return (
        jnp.dot(weights, value, preferred_element_type=F32),
        wide[:, :half] + wide[:, half:],
    )


def kept(at, width, key_base, begin):
    key = key_base + lax.broadcasted_iota(jnp.int32, (at.shape[0], width), 1)
    return (key <= at) & (key >= begin)


def q_body(head_dim, starts, gain, trig, kv, tok, qw, gw_in, q_out, gate, num, den, gw, sem):
    rows = tok.shape[0]
    heads = qw.shape[1] // head_dim
    copy = pltpu.make_async_copy(gw_in, gw, sem)
    copy.start()
    for i in range(heads):
        at = pl.ds(i * rows, rows)
        columns = slice(i * head_dim, (i + 1) * head_dim)
        query = jnp.dot(tok[...], qw[:, columns], preferred_element_type=F32)
        front, back = normed_rotated(query, gain[...], trig[:, :128], trig[:, 128:], head_dim // 8)
        q_out[at, :128] = front.astype(BF16)
        q_out[at, 128:] = back.astype(BF16)
    base = lax.axis_index("seq") * rows
    at = rows_from(base, rows)
    keep = kept(at, rows, base, doc_begin(starts[...], at))
    copy.wait()
    for i in range(heads):
        columns = slice(i * head_dim, (i + 1) * head_dim)
        logits = jnp.dot(tok[...], gw[:, columns], preferred_element_type=F32)
        gate[pl.ds(i * rows, rows), :] = 1.0 / (1.0 + jnp.exp(-logits))
    weighted, sums = attend(
        q_out[...], kv[:, :head_dim], kv[:, head_dim:], keep, head_dim ** (-0.5)
    )
    num[...] = weighted
    den[...] = sums


def source_mask(starts, readers, at, width, source):
    span = readers.shape[0]
    distance = lax.axis_index("seq") - source
    inside = (source >= 0) & (distance >= 1) & (distance <= span)
    listed = readers[jnp.clip(distance - 1, 0, span - 1), jnp.maximum(source, 0)]
    first = jnp.where(inside & (listed == 1), 0, 1 << 30)
    begin = doc_begin(starts[...], at)
    return kept(at, width, source * width, jnp.maximum(begin, first))


def near_body(head_dim, starts, readers, query, num_in, den_in, near, own, num, den):
    rows = near.shape[0]
    block = lax.axis_index("seq")
    at = rows_from(block * rows, rows)

    def add(keys, source, num_in, den_in):
        keep = source_mask(starts, readers, at, rows, source)
        weighted, sums = attend(
            query[...], keys[:, :head_dim], keys[:, head_dim:], keep, head_dim ** (-0.5)
        )
        num[...] = num_in[...] + weighted
        den[...] = den_in[...] + sums

    add(near, block - 2, num_in, den_in)

    @pl.when(lax.rem(block, 2) == 1)
    def _():
        add(own, block - 1, num, den)


def out_body(head_dim, steps, starts, readers, query, gate, num, den, far, ow, *parts):
    rows = far.shape[0]
    heads = query.shape[0] // rows
    block = lax.axis_index("seq")
    core = lax.rem(block, 2)
    head = lax.axis_index("head")
    count = len(ORDER)
    piece = rows // count
    even = lax.rem(head + core, 2) == 0
    firsts = [
        pl.multiple_of(lax.rem(head + jnp.where(even, step, count - step), count) * piece, piece)
        for step in steps
    ]

    def gathered(ref):
        return jnp.concatenate(
            [ref[pl.ds(i * rows + first, piece), :] for i in range(heads) for first in firsts]
        )

    at = jnp.concatenate([rows_from(block * rows + first, piece) for first in firsts])
    keep = source_mask(starts, readers, at, rows, block - 1 - 2 * core)
    weighted, sums = attend(
        gathered(query), far[:, :head_dim], far[:, head_dim:], keep, head_dim ** (-0.5)
    )
    total = jnp.sum(gathered(den) + sums, axis=1, keepdims=True)
    gated = ((gathered(num) + weighted) / total * gathered(gate)).astype(BF16)
    n = len(steps) * piece
    result = sum(
        jnp.dot(
            gated[i * n : (i + 1) * n],
            ow[i * head_dim : (i + 1) * head_dim, :],
            preferred_element_type=F32,
        )
        for i in range(heads)
    ).astype(BF16)
    first = 0
    for ref in parts:
        ref[...] = result[first : first + ref.shape[0], :]
        first += ref.shape[0]


ORDER = (1, 3, 7, 5, 4, 6, 2, 0)


def first_body(rest, got_a, got_c, out):
    piece = out.shape[0]
    total = rest[:piece, :].astype(F32) + got_a[piece:, :].astype(F32) + got_c[...].astype(F32)
    out[...] = total.astype(BF16)


def second_body(rest, got_b, out):
    piece = out.shape[0]
    total = rest[piece : 2 * piece, :].astype(F32) + got_b[piece:, :].astype(F32)
    out[...] = total.astype(BF16)


def last_body(rest, got_a, got_b, first, second, out):
    piece = out.shape[0]
    total = rest[2 * piece :, :].astype(F32)
    for ref in (got_a, got_b, first, second):
        total = total + ref[:piece, :].astype(F32)
    out[...] = total.astype(BF16)


def shards(
    tokens,
    q_weight,
    gate_weight,
    k_weight,
    v_weight,
    q_gain,
    k_gain,
    out_weight,
    doc_starts,
    readers,
):
    rows, width = tokens.shape
    head_dim = q_gain.shape[0]
    heads = q_weight.shape[1] // head_dim
    kv_count = k_weight.shape[1] // head_dim
    kv_share = lax.axis_size("head") // kv_count
    seq, head = lax.axis_size("seq"), lax.axis_size("head")
    starts = doc_starts.reshape(1, -1)
    stacked = heads * rows

    def shape(r, c, dtype=BF16):
        return jax.ShapeDtypeStruct((r, c), dtype)

    def held(r, c, dtype=BF16):
        return pltpu.VMEM((r, c), dtype)

    def far_away(*arrays):
        return tuple(pltpu.with_memory_space_constraint(x, pltpu.HBM) for x in arrays)

    own, trig, near_tokens, near_q = pl.pallas_call(
        functools.partial(kv_body, head_dim, kv_share),
        out_shape=(
            held(rows, 2 * head_dim),
            held(rows, 256, F32),
            held(rows, width),
            held(*q_weight.shape),
        ),
        in_specs=[HBM] * 6,
        out_specs=(VMEM,) * 4,
        scratch_shapes=[
            pltpu.VMEM(starts.shape, jnp.int32),
            pltpu.VMEM((1, head_dim), F32),
            pltpu.VMEM((width, head_dim), BF16),
            pltpu.VMEM((width, head_dim), BF16),
            pltpu.SemaphoreType.DMA((8,)),
        ],
        compiler_params=params(16),
        cost_estimate=cost(4 * rows * width * head_dim, 5 << 20),
        name="kv",
    )(
        *far_away(
            starts, k_gain.reshape(1, -1), tokens, k_weight, v_weight, q_weight
        )
    )

    near = lax.ppermute(own, "seq", [(i, i + 2) for i in range(seq - 2)])
    below = lax.ppermute(own, "seq", [(i, i ^ 1) for i in range(seq)])

    query, gate, num, den = pl.pallas_call(
        functools.partial(q_body, head_dim),
        out_shape=(
            held(stacked, head_dim),
            held(stacked, head_dim, F32),
            held(stacked, head_dim, F32),
            held(stacked, 128, F32),
        ),
        in_specs=[VMEM] * 6 + [HBM],
        out_specs=(VMEM,) * 4,
        scratch_shapes=[pltpu.VMEM(gate_weight.shape, BF16), pltpu.SemaphoreType.DMA],
        compiler_params=params(24),
        cost_estimate=cost(4 * rows * width * heads * head_dim, 5 << 20),
        name="query",
    )(starts, q_gain.reshape(1, -1), trig, own, near_tokens, near_q, *far_away(gate_weight))

    near, query = lax.optimization_barrier((near, query))
    far = lax.ppermute(near, "seq", [(i, i ^ 1) for i in range(seq)])

    table = readers.T
    num, den = pl.pallas_call(
        functools.partial(near_body, head_dim),
        out_shape=(held(stacked, head_dim, F32), held(stacked, 128, F32)),
        in_specs=[VMEM, SMEM] + [VMEM] * 5,
        out_specs=(VMEM,) * 2,
        compiler_params=params(16),
        cost_estimate=cost(4 * stacked * rows * head_dim, 3 << 20),
        name="near",
    )(starts, table, query, num, den, near, below)

    piece = rows // head

    def made(steps, *sizes):
        return pl.pallas_call(
            functools.partial(out_body, head_dim, steps),
            out_shape=tuple(held(n * piece, width) for n in sizes),
            in_specs=[VMEM, SMEM] + [VMEM] * 6,
            out_specs=(VMEM,) * len(sizes),
            compiler_params=params(24),
            cost_estimate=cost(2 * len(steps) * piece * width * heads * head_dim, 4 << 20),
        )(starts, table, query, gate, num, den, far, out_weight)

    def turn(block, step):
        route = []
        for s in range(seq):
            for h in range(head):
                to = (h + step) % head if (s + h) % 2 == 0 else (h - step) % head
                route.append((s * head + h, s * head + to))
        return lax.ppermute(block, ("seq", "head"), route)

    def summed(body, *blocks):
        return pl.pallas_call(
            body,
            out_shape=held(piece, width),
            in_specs=[VMEM] * len(blocks),
            out_specs=VMEM,
            compiler_params=params(8),
            cost_estimate=cost(4 * piece * width, 8 * piece * width),
        )(*blocks)

    (part_a,) = made(ORDER[:2], 2)
    got_a = turn(part_a, 1)
    part_b, part_c, rest = made(ORDER[2:], 2, 1, 3)
    got_c = turn(part_c, -2)
    got_b = turn(part_b, -1)
    first = turn(summed(first_body, rest, got_a, got_c), -2)
    second = turn(summed(second_body, rest, got_b), 2)
    return pl.pallas_call(
        last_body,
        out_shape=shape(piece, width),
        in_specs=[VMEM] * 5,
        out_specs=VMEM,
        compiler_params=params(8),
        name="last",
    )(rest, got_a, got_b, first, second)


def solution(mesh):
    placed = (
        P("seq", None),
        P(None, "head"),
        P(None, "head"),
        P(),
        P(),
        P(),
        P(),
        P("head", None),
        P(),
        P(),
    )
    return jax.shard_map(
        shards, mesh=mesh, in_specs=placed, out_specs=P(("seq", "head"), None), check_vma=False
    )
```

```python
import functools
import math

import jax
import jax.numpy as jnp
from jax import lax
from jax.experimental import pallas as pl
from jax.experimental.pallas import tpu as pltpu
from jax.sharding import PartitionSpec as P


ROPE_THETA = 10000000.0
EPSILON = 1e-06

F32 = jnp.float32
BF16 = jnp.bfloat16
HBM = pl.BlockSpec(memory_space=pltpu.HBM)
VMEM = pl.BlockSpec(memory_space=pltpu.VMEM)
SMEM = pl.BlockSpec(memory_space=pltpu.SMEM)


def params(mib):
    return pltpu.CompilerParams(vmem_limit_bytes=int(mib * (1 << 20)))


def cost(flops, nbytes, trans=0):
    return pl.CostEstimate(flops=flops, bytes_accessed=nbytes, transcendentals=trans)


def rope_angles(offset, head_dim):
    rot_width = head_dim // 4
    half = rot_width // 2
    lane = lax.broadcasted_iota(jnp.int32, (1, 128), 1)
    exponent = lax.rem(lane, half).astype(F32) * (-math.log(ROPE_THETA) * 2.0 / rot_width)
    frequency = jnp.where(lane < rot_width, jnp.exp(exponent), 0.0)
    angle = offset * frequency
    return jnp.cos(angle), jnp.sin(angle) * jnp.where(lane < half, -1.0, 1.0)


def rows_from(base, rows):
    return base + lax.broadcasted_iota(jnp.int32, (rows, 1), 0)


def doc_begin(starts, at):
    return jnp.max(jnp.where(starts <= at, starts, 0), axis=1, keepdims=True)


def normed_rotated(x, gain, cosine, sine, half):
    square = jnp.mean(x * x, axis=-1, keepdims=True)
    x = x * lax.rsqrt(square + EPSILON) * gain
    front = x[:, :128]
    lane = lax.broadcasted_iota(jnp.int32, front.shape, 1)
    partner = jnp.where(
        lane < half, pltpu.roll(front, 128 - half, 1), pltpu.roll(front, half, 1)
    )
    return front * cosine + partner * sine, x[:, 128:]


def kv_body(head_dim, kv_share, starts_in, gain_in, tok_in, kw_in, vw_in, qw_in, kv, trig, tok, qw, starts, gain, kw, vw, sems):
    rows = tok.shape[0]
    column = pl.multiple_of((lax.axis_index("head") // kv_share) * head_dim, head_dim)
    columns = pl.ds(column, head_dim)
    half = tok.shape[1] // 2
    low, high = pl.ds(0, half), pl.ds(half, half)
    pairs = (
        (starts_in, starts),
        (gain_in, gain),
        (tok_in.at[:, low], tok.at[:, low]),
        (kw_in.at[low, columns], kw.at[low, :]),
        (tok_in.at[:, high], tok.at[:, high]),
        (kw_in.at[high, columns], kw.at[high, :]),
        (vw_in.at[:, columns], vw),
        (qw_in, qw),
    )
    copies = [pltpu.make_async_copy(a, b, sems.at[i]) for i, (a, b) in enumerate(pairs)]
    for c in copies:
        c.start()
    base = lax.axis_index("seq") * rows
    copies[0].wait()
    at = rows_from(base, rows)
    offset = (at - doc_begin(starts[...], at)).astype(F32)
    cosine, sine = rope_angles(offset, head_dim)
    trig[:, :128] = cosine
    trig[:, 128:] = sine
    for c in copies[1:4]:
        c.wait()
    key = jnp.dot(tok[:, :half], kw[:half, :], preferred_element_type=F32)
    for c in copies[4:6]:
        c.wait()
    key = key + jnp.dot(tok[:, half:], kw[half:, :], preferred_element_type=F32)
    copies[6].wait()
    kv[:, head_dim:] = jnp.dot(tok[...], vw[...], preferred_element_type=F32).astype(BF16)
    front, back = normed_rotated(key, gain[...], trig[:, :128], trig[:, 128:], head_dim // 8)
    kv[:, :128] = front.astype(BF16)
    kv[:, 128:head_dim] = back.astype(BF16)
    copies[7].wait()


def attend(query, key, value, keep, scale):
    scores = lax.dot_general(query, key, (((1,), (1,)), ((), ())), preferred_element_type=F32)
    rows = keep.shape[0]
    weights = jnp.concatenate(
        [
            jnp.where(keep, jnp.exp(scores[i : i + rows] * scale), 0.0)
            for i in range(0, query.shape[0], rows)
        ]
    ).astype(BF16)
    wide = weights.astype(F32)
    half = wide.shape[1] // 2
    return (
        jnp.dot(weights, value, preferred_element_type=F32),
        wide[:, :half] + wide[:, half:],
    )


def kept(at, width, key_base, begin):
    key = key_base + lax.broadcasted_iota(jnp.int32, (at.shape[0], width), 1)
    return (key <= at) & (key >= begin)


def q_body(head_dim, starts, gain, trig, kv, tok, qw, gw_in, q_out, gate, num, den, gw, sem):
    rows = tok.shape[0]
    heads = qw.shape[1] // head_dim
    copy = pltpu.make_async_copy(gw_in, gw, sem)
    copy.start()
    for i in range(heads):
        at = pl.ds(i * rows, rows)
        columns = slice(i * head_dim, (i + 1) * head_dim)
        query = jnp.dot(tok[...], qw[:, columns], preferred_element_type=F32)
        front, back = normed_rotated(query, gain[...], trig[:, :128], trig[:, 128:], head_dim // 8)
        q_out[at, :128] = front.astype(BF16)
        q_out[at, 128:] = back.astype(BF16)
    base = lax.axis_index("seq") * rows
    at = rows_from(base, rows)
    keep = kept(at, rows, base, doc_begin(starts[...], at))
    copy.wait()
    for i in range(heads):
        columns = slice(i * head_dim, (i + 1) * head_dim)
        logits = jnp.dot(tok[...], gw[:, columns], preferred_element_type=F32)
        gate[pl.ds(i * rows, rows), :] = 1.0 / (1.0 + jnp.exp(-logits))
    weighted, sums = attend(
        q_out[...], kv[:, :head_dim], kv[:, head_dim:], keep, head_dim ** (-0.5)
    )
    num[...] = weighted
    den[...] = sums


def source_mask(starts, readers, at, width, source):
    span = readers.shape[0]
    distance = lax.axis_index("seq") - source
    inside = (source >= 0) & (distance >= 1) & (distance <= span)
    listed = readers[jnp.clip(distance - 1, 0, span - 1), jnp.maximum(source, 0)]
    first = jnp.where(inside & (listed == 1), 0, 1 << 30)
    begin = doc_begin(starts[...], at)
    return kept(at, width, source * width, jnp.maximum(begin, first))


def near_body(head_dim, starts, readers, query, num_in, den_in, near, own, num, den):
    rows = near.shape[0]
    block = lax.axis_index("seq")
    at = rows_from(block * rows, rows)

    def add(keys, source, num_in, den_in):
        keep = source_mask(starts, readers, at, rows, source)
        weighted, sums = attend(
            query[...], keys[:, :head_dim], keys[:, head_dim:], keep, head_dim ** (-0.5)
        )
        num[...] = num_in[...] + weighted
        den[...] = den_in[...] + sums

    add(near, block - 2, num_in, den_in)

    @pl.when(lax.rem(block, 2) == 1)
    def _():
        add(own, block - 1, num, den)


def out_body(head_dim, steps, starts, readers, query, gate, num, den, far, ow, *parts):
    rows = far.shape[0]
    heads = query.shape[0] // rows
    block = lax.axis_index("seq")
    core = lax.rem(block, 2)
    head = lax.axis_index("head")
    count = len(ORDER)
    piece = rows // count
    even = lax.rem(head + core, 2) == 0
    firsts = [
        pl.multiple_of(lax.rem(head + jnp.where(even, step, count - step), count) * piece, piece)
        for step in steps
    ]

    def gathered(ref):
        return jnp.concatenate(
            [ref[pl.ds(i * rows + first, piece), :] for i in range(heads) for first in firsts]
        )

    at = jnp.concatenate([rows_from(block * rows + first, piece) for first in firsts])
    keep = source_mask(starts, readers, at, rows, block - 1 - 2 * core)
    weighted, sums = attend(
        gathered(query), far[:, :head_dim], far[:, head_dim:], keep, head_dim ** (-0.5)
    )
    total = jnp.sum(gathered(den) + sums, axis=1, keepdims=True)
    gated = ((gathered(num) + weighted) / total * gathered(gate)).astype(BF16)
    n = len(steps) * piece
    result = sum(
        jnp.dot(
            gated[i * n : (i + 1) * n],
            ow[i * head_dim : (i + 1) * head_dim, :],
            preferred_element_type=F32,
        )
        for i in range(heads)
    ).astype(BF16)
    first = 0
    for ref in parts:
        ref[...] = result[first : first + ref.shape[0], :]
        first += ref.shape[0]


ORDER = (1, 3, 7, 5, 4, 6, 2, 0)


def first_body(rest, got_a, out):
    piece = out.shape[0]
    total = rest[:piece, :].astype(F32) + got_a[piece:, :].astype(F32)
    out[...] = total.astype(BF16)


def second_body(rest, got_b, got_c, out):
    piece = out.shape[0]
    total = rest[piece : 2 * piece, :].astype(F32)
    total = total + got_b[piece:, :].astype(F32) + got_c[...].astype(F32)
    out[...] = total.astype(BF16)


def last_body(rest, got_a, got_b, first, second, out):
    piece = out.shape[0]
    total = rest[2 * piece :, :].astype(F32)
    for ref in (got_a, got_b, first, second):
        total = total + ref[:piece, :].astype(F32)
    out[...] = total.astype(BF16)


def shards(
    tokens,
    q_weight,
    gate_weight,
    k_weight,
    v_weight,
    q_gain,
    k_gain,
    out_weight,
    doc_starts,
    readers,
):
    rows, width = tokens.shape
    head_dim = q_gain.shape[0]
    heads = q_weight.shape[1] // head_dim
    kv_count = k_weight.shape[1] // head_dim
    kv_share = lax.axis_size("head") // kv_count
    seq, head = lax.axis_size("seq"), lax.axis_size("head")
    starts = doc_starts.reshape(1, -1)
    stacked = heads * rows

    def shape(r, c, dtype=BF16):
        return jax.ShapeDtypeStruct((r, c), dtype)

    def held(r, c, dtype=BF16):
        return pltpu.VMEM((r, c), dtype)

    def far_away(*arrays):
        return tuple(pltpu.with_memory_space_constraint(x, pltpu.HBM) for x in arrays)

    own, trig, near_tokens, near_q = pl.pallas_call(
        functools.partial(kv_body, head_dim, kv_share),
        out_shape=(
            held(rows, 2 * head_dim),
            held(rows, 256, F32),
            held(rows, width),
            held(*q_weight.shape),
        ),
        in_specs=[HBM] * 6,
        out_specs=(VMEM,) * 4,
        scratch_shapes=[
            pltpu.VMEM(starts.shape, jnp.int32),
            pltpu.VMEM((1, head_dim), F32),
            pltpu.VMEM((width, head_dim), BF16),
            pltpu.VMEM((width, head_dim), BF16),
            pltpu.SemaphoreType.DMA((8,)),
        ],
        compiler_params=params(16),
        cost_estimate=cost(4 * rows * width * head_dim, 5 << 20),
        name="kv",
    )(
        *far_away(
            starts, k_gain.reshape(1, -1), tokens, k_weight, v_weight, q_weight
        )
    )

    near = lax.ppermute(own, "seq", [(i, i + 2) for i in range(seq - 2)])
    below = lax.ppermute(own, "seq", [(i, i ^ 1) for i in range(seq)])

    query, gate, num, den = pl.pallas_call(
        functools.partial(q_body, head_dim),
        out_shape=(
            held(stacked, head_dim),
            held(stacked, head_dim, F32),
            held(stacked, head_dim, F32),
            held(stacked, 128, F32),
        ),
        in_specs=[VMEM] * 6 + [HBM],
        out_specs=(VMEM,) * 4,
        scratch_shapes=[pltpu.VMEM(gate_weight.shape, BF16), pltpu.SemaphoreType.DMA],
        compiler_params=params(24),
        cost_estimate=cost(4 * rows * width * heads * head_dim, 5 << 20),
        name="query",
    )(starts, q_gain.reshape(1, -1), trig, own, near_tokens, near_q, *far_away(gate_weight))

    near, query = lax.optimization_barrier((near, query))
    far = lax.ppermute(near, "seq", [(i, i ^ 1) for i in range(seq)])

    table = readers.T
    num, den = pl.pallas_call(
        functools.partial(near_body, head_dim),
        out_shape=(held(stacked, head_dim, F32), held(stacked, 128, F32)),
        in_specs=[VMEM, SMEM] + [VMEM] * 5,
        out_specs=(VMEM,) * 2,
        compiler_params=params(16),
        cost_estimate=cost(4 * stacked * rows * head_dim, 3 << 20),
        name="near",
    )(starts, table, query, num, den, near, below)

    piece = rows // head

    def made(steps, *sizes):
        return pl.pallas_call(
            functools.partial(out_body, head_dim, steps),
            out_shape=tuple(held(n * piece, width) for n in sizes),
            in_specs=[VMEM, SMEM] + [VMEM] * 6,
            out_specs=(VMEM,) * len(sizes),
            compiler_params=params(24),
            cost_estimate=cost(2 * len(steps) * piece * width * heads * head_dim, 4 << 20),
        )(starts, table, query, gate, num, den, far, out_weight)

    def turn(block, step):
        route = []
        for s in range(seq):
            for h in range(head):
                to = (h + step) % head if (s + h) % 2 == 0 else (h - step) % head
                route.append((s * head + h, s * head + to))
        return lax.ppermute(block, ("seq", "head"), route)

    def summed(body, *blocks):
        return pl.pallas_call(
            body,
            out_shape=held(piece, width),
            in_specs=[VMEM] * len(blocks),
            out_specs=VMEM,
            compiler_params=params(8),
            cost_estimate=cost(4 * piece * width, 8 * piece * width),
        )(*blocks)

    part_a, part_b, part_c, rest = made(ORDER, 2, 2, 1, 3)
    got_a = turn(part_a, 1)
    got_c = turn(part_c, 2)
    got_b = turn(part_b, -1)
    first = turn(summed(first_body, rest, got_a), -2)
    second = turn(summed(second_body, rest, got_b, got_c), 2)
    return pl.pallas_call(
        last_body,
        out_shape=shape(piece, width),
        in_specs=[VMEM] * 5,
        out_specs=VMEM,
        compiler_params=params(8),
        name="last",
    )(rest, got_a, got_b, first, second)


def solution(mesh):
    placed = (
        P("seq", None),
        P(None, "head"),
        P(None, "head"),
        P(),
        P(),
        P(),
        P(),
        P("head", None),
        P(),
        P(),
    )
    return jax.shard_map(
        shards, mesh=mesh, in_specs=placed, out_specs=P(("seq", "head"), None), check_vma=False
    )
```

```python
import functools
import math

import jax
import jax.numpy as jnp
from jax import lax
from jax.experimental import pallas as pl
from jax.experimental.pallas import tpu as pltpu
from jax.sharding import PartitionSpec as P


ROPE_THETA = 10000000.0
EPSILON = 1e-06

F32 = jnp.float32
BF16 = jnp.bfloat16
HBM = pl.BlockSpec(memory_space=pltpu.HBM)
VMEM = pl.BlockSpec(memory_space=pltpu.VMEM)
SMEM = pl.BlockSpec(memory_space=pltpu.SMEM)


def params(mib):
    return pltpu.CompilerParams(vmem_limit_bytes=int(mib * (1 << 20)))


def cost(flops, nbytes, trans=0):
    return pl.CostEstimate(flops=flops, bytes_accessed=nbytes, transcendentals=trans)


def rope_angles(offset, head_dim):
    rot_width = head_dim // 4
    half = rot_width // 2
    lane = lax.broadcasted_iota(jnp.int32, (1, 128), 1)
    exponent = lax.rem(lane, half).astype(F32) * (-math.log(ROPE_THETA) * 2.0 / rot_width)
    frequency = jnp.where(lane < rot_width, jnp.exp(exponent), 0.0)
    angle = offset * frequency
    return jnp.cos(angle), jnp.sin(angle) * jnp.where(lane < half, -1.0, 1.0)


def rows_from(base, rows):
    return base + lax.broadcasted_iota(jnp.int32, (rows, 1), 0)


def doc_begin(starts, at):
    return jnp.max(jnp.where(starts <= at, starts, 0), axis=1, keepdims=True)


def normed_rotated(x, gain, cosine, sine, half):
    square = jnp.mean(x * x, axis=-1, keepdims=True)
    x = x * lax.rsqrt(square + EPSILON) * gain
    front = x[:, :128]
    lane = lax.broadcasted_iota(jnp.int32, front.shape, 1)
    partner = jnp.where(
        lane < half, pltpu.roll(front, 128 - half, 1), pltpu.roll(front, half, 1)
    )
    return front * cosine + partner * sine, x[:, 128:]


def kv_body(head_dim, kv_share, starts_in, gain_in, tok_in, kw_in, vw_in, qw_in, kv, trig, tok, qw, starts, gain, kw, vw, sems):
    rows = tok.shape[0]
    column = pl.multiple_of((lax.axis_index("head") // kv_share) * head_dim, head_dim)
    columns = pl.ds(column, head_dim)
    half = tok.shape[1] // 2
    low, high = pl.ds(0, half), pl.ds(half, half)
    pairs = (
        (starts_in, starts),
        (gain_in, gain),
        (tok_in.at[:, low], tok.at[:, low]),
        (kw_in.at[low, columns], kw.at[low, :]),
        (tok_in.at[:, high], tok.at[:, high]),
        (kw_in.at[high, columns], kw.at[high, :]),
        (vw_in.at[:, columns], vw),
        (qw_in, qw),
    )
    copies = [pltpu.make_async_copy(a, b, sems.at[i]) for i, (a, b) in enumerate(pairs)]
    for c in copies:
        c.start()
    base = lax.axis_index("seq") * rows
    copies[0].wait()
    at = rows_from(base, rows)
    offset = (at - doc_begin(starts[...], at)).astype(F32)
    cosine, sine = rope_angles(offset, head_dim)
    trig[:, :128] = cosine
    trig[:, 128:] = sine
    for c in copies[1:4]:
        c.wait()
    key = jnp.dot(tok[:, :half], kw[:half, :], preferred_element_type=F32)
    for c in copies[4:6]:
        c.wait()
    key = key + jnp.dot(tok[:, half:], kw[half:, :], preferred_element_type=F32)
    copies[6].wait()
    kv[:, head_dim:] = jnp.dot(tok[...], vw[...], preferred_element_type=F32).astype(BF16)
    front, back = normed_rotated(key, gain[...], trig[:, :128], trig[:, 128:], head_dim // 8)
    kv[:, :128] = front.astype(BF16)
    kv[:, 128:head_dim] = back.astype(BF16)
    copies[7].wait()


def attend(query, key, value, keep, scale):
    scores = lax.dot_general(query, key, (((1,), (1,)), ((), ())), preferred_element_type=F32)
    rows = keep.shape[0]
    weights = jnp.concatenate(
        [
            jnp.where(keep, jnp.exp(scores[i : i + rows] * scale), 0.0)
            for i in range(0, query.shape[0], rows)
        ]
    ).astype(BF16)
    wide = weights.astype(F32)
    half = wide.shape[1] // 2
    return (
        jnp.dot(weights, value, preferred_element_type=F32),
        wide[:, :half] + wide[:, half:],
    )


def kept(at, width, key_base, begin):
    key = key_base + lax.broadcasted_iota(jnp.int32, (at.shape[0], width), 1)
    return (key <= at) & (key >= begin)


def q_body(head_dim, starts, gain, trig, kv, tok, qw, gw_in, q_out, gate, num, den, gw, sem):
    rows = tok.shape[0]
    heads = qw.shape[1] // head_dim
    copy = pltpu.make_async_copy(gw_in, gw, sem)
    copy.start()
    for i in range(heads):
        at = pl.ds(i * rows, rows)
        columns = slice(i * head_dim, (i + 1) * head_dim)
        query = jnp.dot(tok[...], qw[:, columns], preferred_element_type=F32)
        front, back = normed_rotated(query, gain[...], trig[:, :128], trig[:, 128:], head_dim // 8)
        q_out[at, :128] = front.astype(BF16)
        q_out[at, 128:] = back.astype(BF16)
    base = lax.axis_index("seq") * rows
    at = rows_from(base, rows)
    keep = kept(at, rows, base, doc_begin(starts[...], at))
    copy.wait()
    for i in range(heads):
        columns = slice(i * head_dim, (i + 1) * head_dim)
        logits = jnp.dot(tok[...], gw[:, columns], preferred_element_type=F32)
        gate[pl.ds(i * rows, rows), :] = 1.0 / (1.0 + jnp.exp(-logits))
    weighted, sums = attend(
        q_out[...], kv[:, :head_dim], kv[:, head_dim:], keep, head_dim ** (-0.5)
    )
    num[...] = weighted
    den[...] = sums


def source_mask(starts, readers, at, width, source):
    span = readers.shape[0]
    distance = lax.axis_index("seq") - source
    inside = (source >= 0) & (distance >= 1) & (distance <= span)
    listed = readers[jnp.clip(distance - 1, 0, span - 1), jnp.maximum(source, 0)]
    first = jnp.where(inside & (listed == 1), 0, 1 << 30)
    begin = doc_begin(starts[...], at)
    return kept(at, width, source * width, jnp.maximum(begin, first))


def near_body(head_dim, starts, readers, query, num_in, den_in, near, own, num, den):
    rows = near.shape[0]
    block = lax.axis_index("seq")
    at = rows_from(block * rows, rows)

    def add(keys, source, num_in, den_in):
        keep = source_mask(starts, readers, at, rows, source)
        weighted, sums = attend(
            query[...], keys[:, :head_dim], keys[:, head_dim:], keep, head_dim ** (-0.5)
        )
        num[...] = num_in[...] + weighted
        den[...] = den_in[...] + sums

    add(near, block - 2, num_in, den_in)

    @pl.when(lax.rem(block, 2) == 1)
    def _():
        add(own, block - 1, num, den)


def out_body(head_dim, steps, starts, readers, query, gate, num, den, far, ow, *parts):
    rows = far.shape[0]
    heads = query.shape[0] // rows
    block = lax.axis_index("seq")
    core = lax.rem(block, 2)
    head = lax.axis_index("head")
    count = len(ORDER)
    piece = rows // count
    even = lax.rem(head + core, 2) == 0
    firsts = [
        pl.multiple_of(lax.rem(head + jnp.where(even, step, count - step), count) * piece, piece)
        for step in steps
    ]

    def gathered(ref):
        return jnp.concatenate(
            [ref[pl.ds(i * rows + first, piece), :] for i in range(heads) for first in firsts]
        )

    at = jnp.concatenate([rows_from(block * rows + first, piece) for first in firsts])
    keep = source_mask(starts, readers, at, rows, block - 1 - 2 * core)
    weighted, sums = attend(
        gathered(query), far[:, :head_dim], far[:, head_dim:], keep, head_dim ** (-0.5)
    )
    total = jnp.sum(gathered(den) + sums, axis=1, keepdims=True)
    gated = ((gathered(num) + weighted) / total * gathered(gate)).astype(BF16)
    n = len(steps) * piece
    result = sum(
        jnp.dot(
            gated[i * n : (i + 1) * n],
            ow[i * head_dim : (i + 1) * head_dim, :],
            preferred_element_type=F32,
        )
        for i in range(heads)
    ).astype(BF16)
    first = 0
    for ref in parts:
        ref[...] = result[first : first + ref.shape[0], :]
        first += ref.shape[0]


ORDER = (1, 3, 7, 5, 4, 6, 2, 0)


def first_body(rest, got_a, out):
    piece = out.shape[0]
    total = rest[:piece, :].astype(F32) + got_a[piece : 2 * piece, :].astype(F32)
    out[...] = total.astype(BF16)


def second_body(rest, got_a, got_b, got_c, out):
    piece = out.shape[0]
    total = rest[piece : 2 * piece, :].astype(F32) + got_a[2 * piece :, :].astype(F32)
    total = total + got_b[...].astype(F32) + got_c[...].astype(F32)
    out[...] = total.astype(BF16)


def last_body(rest, got_a, first, second, out):
    piece = out.shape[0]
    total = rest[2 * piece :, :].astype(F32)
    for ref in (got_a, first, second):
        total = total + ref[:piece, :].astype(F32)
    out[...] = total.astype(BF16)


def shards(
    tokens,
    q_weight,
    gate_weight,
    k_weight,
    v_weight,
    q_gain,
    k_gain,
    out_weight,
    doc_starts,
    readers,
):
    rows, width = tokens.shape
    head_dim = q_gain.shape[0]
    heads = q_weight.shape[1] // head_dim
    kv_count = k_weight.shape[1] // head_dim
    kv_share = lax.axis_size("head") // kv_count
    seq, head = lax.axis_size("seq"), lax.axis_size("head")
    starts = doc_starts.reshape(1, -1)
    stacked = heads * rows

    def shape(r, c, dtype=BF16):
        return jax.ShapeDtypeStruct((r, c), dtype)

    def held(r, c, dtype=BF16):
        return pltpu.VMEM((r, c), dtype)

    def far_away(*arrays):
        return tuple(pltpu.with_memory_space_constraint(x, pltpu.HBM) for x in arrays)

    own, trig, near_tokens, near_q = pl.pallas_call(
        functools.partial(kv_body, head_dim, kv_share),
        out_shape=(
            held(rows, 2 * head_dim),
            held(rows, 256, F32),
            held(rows, width),
            held(*q_weight.shape),
        ),
        in_specs=[HBM] * 6,
        out_specs=(VMEM,) * 4,
        scratch_shapes=[
            pltpu.VMEM(starts.shape, jnp.int32),
            pltpu.VMEM((1, head_dim), F32),
            pltpu.VMEM((width, head_dim), BF16),
            pltpu.VMEM((width, head_dim), BF16),
            pltpu.SemaphoreType.DMA((8,)),
        ],
        compiler_params=params(16),
        cost_estimate=cost(4 * rows * width * head_dim, 5 << 20),
        name="kv",
    )(
        *far_away(
            starts, k_gain.reshape(1, -1), tokens, k_weight, v_weight, q_weight
        )
    )

    near = lax.ppermute(own, "seq", [(i, i + 2) for i in range(seq - 2)])
    below = lax.ppermute(own, "seq", [(i, i ^ 1) for i in range(seq)])

    query, gate, num, den = pl.pallas_call(
        functools.partial(q_body, head_dim),
        out_shape=(
            held(stacked, head_dim),
            held(stacked, head_dim, F32),
            held(stacked, head_dim, F32),
            held(stacked, 128, F32),
        ),
        in_specs=[VMEM] * 6 + [HBM],
        out_specs=(VMEM,) * 4,
        scratch_shapes=[pltpu.VMEM(gate_weight.shape, BF16), pltpu.SemaphoreType.DMA],
        compiler_params=params(24),
        cost_estimate=cost(4 * rows * width * heads * head_dim, 5 << 20),
        name="query",
    )(starts, q_gain.reshape(1, -1), trig, own, near_tokens, near_q, *far_away(gate_weight))

    near, query = lax.optimization_barrier((near, query))
    far = lax.ppermute(near, "seq", [(i, i ^ 1) for i in range(seq)])

    table = readers.T
    num, den = pl.pallas_call(
        functools.partial(near_body, head_dim),
        out_shape=(held(stacked, head_dim, F32), held(stacked, 128, F32)),
        in_specs=[VMEM, SMEM] + [VMEM] * 5,
        out_specs=(VMEM,) * 2,
        compiler_params=params(16),
        cost_estimate=cost(4 * stacked * rows * head_dim, 3 << 20),
        name="near",
    )(starts, table, query, num, den, near, below)

    piece = rows // head

    def made(steps, *sizes):
        return pl.pallas_call(
            functools.partial(out_body, head_dim, steps),
            out_shape=tuple(held(n * piece, width) for n in sizes),
            in_specs=[VMEM, SMEM] + [VMEM] * 6,
            out_specs=(VMEM,) * len(sizes),
            compiler_params=params(24),
            cost_estimate=cost(2 * len(steps) * piece * width * heads * head_dim, 4 << 20),
        )(starts, table, query, gate, num, den, far, out_weight)

    def turn(block, step):
        route = []
        for s in range(seq):
            for h in range(head):
                to = (h + step) % head if (s + h) % 2 == 0 else (h - step) % head
                route.append((s * head + h, s * head + to))
        return lax.ppermute(block, ("seq", "head"), route)

    def summed(body, *blocks):
        return pl.pallas_call(
            body,
            out_shape=held(piece, width),
            in_specs=[VMEM] * len(blocks),
            out_specs=VMEM,
            compiler_params=params(8),
            cost_estimate=cost(4 * piece * width, 8 * piece * width),
        )(*blocks)

    part_a, part_b, part_c, rest = made(ORDER, 3, 1, 1, 3)
    got_a = turn(part_a, 1)
    got_c = turn(part_c, 2)
    got_b = turn(part_b, -1)
    first = turn(summed(first_body, rest, got_a), -2)
    second = turn(summed(second_body, rest, got_a, got_b, got_c), 2)
    return pl.pallas_call(
        last_body,
        out_shape=shape(piece, width),
        in_specs=[VMEM] * 4,
        out_specs=VMEM,
        compiler_params=params(8),
        name="last",
    )(rest, got_a, first, second)


def solution(mesh):
    placed = (
        P("seq", None),
        P(None, "head"),
        P(None, "head"),
        P(),
        P(),
        P(),
        P(),
        P("head", None),
        P(),
        P(),
    )
    return jax.shard_map(
        shards, mesh=mesh, in_specs=placed, out_specs=P(("seq", "head"), None), check_vma=False
    )
```
